32 devices in a mesh: sec: 4 (over x, core), row: 4 (over z), col: 2 (over y).
Axes of the slice: x: 2, y: 2, z: 4, core: 2. Of those that a mesh axis runs over, the one named last changes fastest.
Arguments:
- images: float32 [4, 1024, 512], P('sec', 'row', 'col'), may hold values from -6 to 6
- stiffness: float32 [4, 1024, 512], P('sec', 'row', 'col'), may hold values from 0.1 to 1
Outputs:
- tensor: float32 [5, 4, 1024, 512], P(None, 'sec', 'row', 'col')
- field: float32 [2, 4, 1024, 512], P(None, 'sec', 'row', 'col')
The draws below stay inside these ranges and needn't reach their ends.
All inputs are finite; a program needn't handle non-finite values.
Results may differ from the reference program's by a relative error of at most 0.00002.
Values sent between devices are 32-bit elements; how exact they have to be, the bound alone decides.
A program may use at most 64 MiB of HBM per device.

```python
import math
import jax
import jax.numpy as jnp

RADIUS = 4
SWEEPS = 4
ROUNDS = 2
SECTIONS = 4
HEIGHT = 1024
WIDTH = 512


def steps_of(rng, extent, pieces, least, high):
    def one(position, blocks):
        heights = jax.random.uniform(jax.random.fold_in(jax.random.fold_in(rng, 6), position), (blocks,), jnp.float32, least / len(pieces), high / len(pieces))
        return jnp.repeat(jnp.exp(heights), extent[position] // blocks).reshape((-1,) + (1,) * (len(extent) - position - 1))

    factor_of = one(*pieces[0])
    for cut in pieces[1:]:
        factor_of = factor_of * one(*cut)
    return factor_of


def scatter_about(key, shape, width, reach, cuts=(), held_as=jnp.bfloat16):
    array = width * jax.random.normal(key, shape, jnp.float32)
    if cuts:
        array = array * steps_of(key, shape, cuts, -0.22, 0.18)
    return jnp.clip(array, -reach, reach).astype(held_as)


def setup_inputs(seed: int = 0) -> dict:
    seeds = jax.random.split(jax.random.key(seed), 3)
    return {
        "images": scatter_about(seeds[0], (SECTIONS, HEIGHT, WIDTH), 1.0, 6.0, ((0, 4), (1, 4), (2, 2)), jnp.float32),
        "stiffness": jnp.clip(jnp.exp(math.log(1.0) - 2.3025851 * jax.random.uniform(seeds[1], (SECTIONS, HEIGHT, WIDTH), jnp.float32) ** steps_of(seeds[1], (SECTIONS, HEIGHT, WIDTH), ((0, 4), (1, 4), (2, 2)), -0.2, 0.2)), 0.1, 1.0),
    }


coupling = 0.25

def gradients(padded):
    grad_y = (padded[..., 2:, 1:-1] - padded[..., :-2, 1:-1]) * 0.5
    grad_x = (padded[..., 1:-1, 2:] - padded[..., 1:-1, :-2]) * 0.5
    return (grad_y, grad_x)

def products(grad_y, grad_x, change):
    return jnp.stack([grad_x * grad_x, grad_x * grad_y, grad_y * grad_y, grad_x * change, grad_y * change])

def window_mean(widened, radius):
    row_count = widened.shape[-2] - 2 * radius
    col_count = widened.shape[-1] - 2 * radius
    partial_rows = widened[..., 0:row_count, :]
    for offset in range(1, 2 * radius + 1):
        partial_rows = partial_rows + widened[..., offset:offset + row_count, :]
    summed = partial_rows[..., 0:col_count]
    for offset in range(1, 2 * radius + 1):
        summed = summed + partial_rows[..., offset:offset + col_count]
    return summed / float((2 * radius + 1) ** 2)

def couplings(stiff_pad):
    centre = stiff_pad[..., 1:-1, 1:-1]
    kappa_up = jnp.sqrt(centre * stiff_pad[..., :-2, 1:-1])
    kappa_down = jnp.sqrt(centre * stiff_pad[..., 2:, 1:-1])
    kappa_left = jnp.sqrt(centre * stiff_pad[..., 1:-1, :-2])
    kappa_right = jnp.sqrt(centre * stiff_pad[..., 1:-1, 2:])
    kappa_sum = kappa_up + kappa_down + kappa_left + kappa_right
    return ((kappa_up, kappa_down, kappa_left, kappa_right), kappa_sum)

def jacobi(field_pad, kappas, kappa_sum, tensor, beside):
    neighbour = kappas[0] * field_pad[..., :-2, 1:-1] + kappas[1] * field_pad[..., 2:, 1:-1]
    neighbour = neighbour + kappas[2] * field_pad[..., 1:-1, :-2] + kappas[3] * field_pad[..., 1:-1, 2:]
    diagonal = kappa_sum + 2.0 * coupling
    first_diag = tensor[0] + diagonal
    second_diag = tensor[2] + diagonal
    off_diag = tensor[1]
    determinant = first_diag * second_diag - off_diag * off_diag
    right_x = coupling * beside[0] + neighbour[0] - tensor[3]
    right_y = coupling * beside[1] + neighbour[1] - tensor[4]
    new_x = (second_diag * right_x - off_diag * right_y) / determinant
    new_y = (first_diag * right_y - off_diag * right_x) / determinant
    return jnp.stack([new_x, new_y])

def reference(images, stiffness):
    section_count = images.shape[0]
    later = jnp.concatenate([images[1:], jnp.zeros_like(images[:1])], axis=0)
    padded = jnp.pad(images, ((0, 0), (1, 1), (1, 1)))
    grad_y, grad_x = gradients(padded)
    stacked = products(grad_y, grad_x, later - images)
    widened = jnp.pad(stacked, ((0, 0), (0, 0), (RADIUS, RADIUS), (RADIUS, RADIUS)))
    tensor = window_mean(widened, RADIUS)
    keep = (jnp.arange(section_count) < section_count - 1).astype(tensor.dtype)
    tensor = tensor * keep[None, :, None, None]
    stiff_pad = jnp.pad(stiffness, ((0, 0), (1, 1), (1, 1)))
    kappas, kappa_sum = couplings(stiff_pad)
    field = jnp.zeros((2,) + images.shape, images.dtype)
    for round_index in range(ROUNDS):
        if round_index == 0:
            beside = jnp.zeros_like(field)
        else:
            below_part = jnp.concatenate([jnp.zeros_like(field[:, :1]), field[:, :-1]], axis=1)
            above_part = jnp.concatenate([field[:, 1:], jnp.zeros_like(field[:, :1])], axis=1)
            beside = below_part + above_part
        for sweep_index in range(SWEEPS):
            field_pad = jnp.pad(field, ((0, 0), (0, 0), (1, 1), (1, 1)))
            field = jacobi(field_pad, kappas, kappa_sum, tensor, beside)
    return (tensor, field)
```

```python
import functools

import jax
import jax.numpy as jnp
from jax import lax
from jax.experimental import pallas as pl
from jax.experimental.pallas import tpu as pltpu
from jax.sharding import PartitionSpec as P

RADIUS = 4
SWEEPS = 4
ROUNDS = 2
COUPLING = 0.25
MESH = pl.DeviceIdType.MESH

LANES = 128
HALO = 16
EDGE = HALO + 8
SLOT = 16
FOLD = LANES // (2 * SLOT)

TILE_B = 0
ROW_A_UP, ROW_A_DOWN, ROW_S_UP, ROW_S_DOWN = 1, 2, 3, 4
COL_RIGHT, COL_LEFT = 5, 6
FWD_TOP, FWD_BOTTOM, FWD_RIGHT, FWD_LEFT = 7, 8, 9, 10
FIELD_NEXT, FIELD_PREV, RIM_NEXT, RIM_PREV = 11, 12, 13, 14
COPIES = 15


def lane_roll(x, shift):
    return pltpu.roll(x, shift % x.shape[1], 1)


def window_sum(x, axis):
    size = x.shape[axis]
    two = x + pltpu.roll(x, 1, axis)
    four = two + pltpu.roll(two, 2, axis)
    return x + (pltpu.roll(four, 1, axis) + pltpu.roll(four, size - 4, axis))


def stacked(block):
    rows = block.shape[0]
    return tuple(
        x[8 : rows - 8, :] for x in (pltpu.roll(block, 1, 0), block, pltpu.roll(block, rows - 1, 0))
    )


def kernel(
    counts, images, stiff, tensor_out, field_out,
    a, b, s, ku, kd, kl, kr, ks, gx, gy, pr, tt, ca, cb, cc, bx, by, f0, f1,
    send_right, send_left, got_left, got_right, next_left, next_right,
    rim, rim_before, rim_after, main_before, main_after,
    local_sem, send_sem, recv_sem,
):
    sec, row, col = (lax.axis_index(name) for name in ("sec", "row", "col"))
    n_sec, n_row, n_col = counts
    rows, width = images.shape[1], images.shape[2]
    total, wide = a.shape
    has_prev, has_next = sec > 0, sec < n_sec - 1
    has_up, has_down = row > 0, row < n_row - 1
    has_left, has_right = col > 0, col < n_col - 1
    sides = (
        (has_prev, (sec - 1, row, col)), (has_next, (sec + 1, row, col)),
        (has_up, (sec, row - 1, col)), (has_down, (sec, row + 1, col)),
        (has_left, (sec, row, col - 1)), (has_right, (sec, row, col + 1)),
    )
    prev_id, next_id, up_id, down_id, left_id, right_id = (side[1] for side in sides)
    end = EDGE + rows
    first, last = 8, total - 8
    inner = pl.ds(EDGE, rows)
    main = pl.ds(0, width)
    top, bottom = pl.ds(EDGE - HALO, HALO), pl.ds(end, HALO)
    piece = (last - first) // FOLD

    def remote(src, dst, k, device):
        return pltpu.make_async_remote_copy(
            src_ref=src, dst_ref=dst, send_sem=send_sem.at[k], recv_sem=recv_sem.at[k],
            device_id=device, device_id_type=MESH,
        )

    load_a = pltpu.make_async_copy(images.at[0], a.at[inner, main], local_sem.at[0])
    load_s = pltpu.make_async_copy(stiff.at[0], s.at[inner, main], local_sem.at[1])
    load_a.start()
    load_s.start()
    barrier = pltpu.get_barrier_semaphore()
    for there, device in sides:
        @pl.when(there)
        def _():
            pl.semaphore_signal(barrier, inc=1, device_id=device, device_id_type=MESH)

    def clear(ref):
        ref[...] = jnp.zeros(ref.shape, jnp.float32)

    @pl.when(jnp.logical_not(has_up))
    def _():
        clear(a.at[top, main])
        clear(s.at[top, main])

    @pl.when(jnp.logical_not(has_down))
    def _():
        clear(a.at[bottom, main])
        clear(s.at[bottom, main])

    @pl.when(jnp.logical_not(has_left))
    def _():
        clear(got_left)

    @pl.when(jnp.logical_not(has_right))
    def _():
        clear(got_right)

    @pl.when(jnp.logical_not(has_next))
    def _():
        clear(b)
        clear(next_left)
        clear(next_right)
        clear(rim_after)
        clear(main_after)

    @pl.when(jnp.logical_not(has_prev))
    def _():
        clear(rim_before)
        clear(main_before)

    for ref in (a, s):
        clear(ref.at[pl.ds(0, 8), :])
        clear(ref.at[pl.ds(total - 8, 8), :])
    for ref in (f0, f1):
        for part in range(2):
            clear(ref.at[part, pl.ds(8, 8), :])
            clear(ref.at[part, pl.ds(total - 16, 8), :])

    pl.semaphore_wait(barrier, sum(jnp.where(there, 1, 0) for there, _device in sides))

    tile_b = remote(images.at[0], b.at[inner, main], TILE_B, prev_id)
    a_up = remote(images.at[0, pl.ds(0, HALO)], a.at[bottom, main], ROW_A_UP, up_id)
    s_up = remote(stiff.at[0, pl.ds(0, HALO)], s.at[bottom, main], ROW_S_UP, up_id)
    a_down = remote(images.at[0, pl.ds(rows - HALO, HALO)], a.at[top, main], ROW_A_DOWN, down_id)
    s_down = remote(stiff.at[0, pl.ds(rows - HALO, HALO)], s.at[top, main], ROW_S_DOWN, down_id)
    fwd_top = remote(a.at[top, main], b.at[top, main], FWD_TOP, prev_id)
    fwd_bottom = remote(a.at[bottom, main], b.at[bottom, main], FWD_BOTTOM, prev_id)
    col_right = remote(send_right, got_left, COL_RIGHT, right_id)
    col_left = remote(send_left, got_right, COL_LEFT, left_id)
    fwd_left = remote(got_left, next_left, FWD_LEFT, prev_id)
    fwd_right = remote(got_right, next_right, FWD_RIGHT, prev_id)

    @pl.when(has_up)
    def _():
        a_up.start()
        s_up.start()

    @pl.when(has_down)
    def _():
        a_down.start()
        s_down.start()

    @pl.when(has_prev)
    def _():
        tile_b.start()

    load_a.wait()
    load_s.wait()

    @pl.when(has_up)
    def _():
        a_down.wait_recv()
        s_down.wait_recv()

    @pl.when(has_down)
    def _():
        a_up.wait_recv()
        s_up.wait_recv()

    @pl.when(has_prev)
    def _():
        fwd_top.start()
        fwd_bottom.start()

    def lanes_of(shape):
        return lax.broadcasted_iota(jnp.int32, shape, 1)

    lane = lanes_of((piece, LANES))

    def packed(ref_low, ref_high, column, at):
        out = jnp.zeros((piece, LANES), jnp.float32)
        for j in range(FOLD):
            span = pl.ds(first + j * piece, piece)
            for k, ref in enumerate((ref_low, ref_high)):
                low = (2 * j + k) * SLOT
                moved = lane_roll(ref[span, column], low - at)
                out = jnp.where((lane >= low) & (lane < low + SLOT), moved, out)
        return out

    def unpack(ref, left, right, k):
        for j in range(FOLD):
            low = (2 * j + k) * SLOT
            span = pl.ds(first + j * piece, piece)
            from_right = jnp.where(lane < SLOT, lane_roll(right[...], -low), 0.0)
            from_left = lane_roll(left[...], LANES - SLOT - low)
            ref[span, pl.ds(width, LANES)] = jnp.where(lane >= LANES - SLOT, from_left, from_right)

    @pl.when(has_right)
    def _():
        send_right[...] = packed(a, s, pl.ds(width - LANES, LANES), LANES - SLOT)
        col_right.start()

    @pl.when(has_left)
    def _():
        send_left[...] = packed(a, s, pl.ds(0, LANES), 0)
        col_left.start()

    @pl.when(has_left)
    def _():
        col_right.wait_recv()

    @pl.when(has_right)
    def _():
        col_left.wait_recv()

    @pl.when(has_prev)
    def _():
        fwd_left.start()
        fwd_right.start()

    unpack(a, got_left, got_right, 0)
    unpack(s, got_left, got_right, 1)

    step = 16

    def blocks(low, high, body):
        def one(i, carry):
            body(pl.multiple_of(low + i * step, 8))
            return carry

        lax.fori_loop(0, (high - low) // step, one, 0)

    lane_wide = lanes_of((step, wide))
    middle = width + LANES // 2
    lane_ok = (
        (lane_wide < width)
        | ((lane_wide < middle) & has_right)
        | ((lane_wide >= middle) & has_left)
    )
    row_in = lax.broadcasted_iota(jnp.int32, (step, wide), 0)

    def gradient_block(r):
        at = pl.ds(r, step)
        rr = row_in + r
        ok = lane_ok & ((rr >= EDGE) | has_up) & ((rr < end) | has_down)
        up, mid, down = stacked(a[pl.ds(r - 8, step + 16), :])
        dx = jnp.where(ok, (lane_roll(mid, -1) - lane_roll(mid, 1)) * 0.5, 0.0)
        dy = jnp.where(ok, (down - up) * 0.5, 0.0)
        gx[at, :] = dx
        gy[at, :] = dy
        pr[0, at, :] = dx * dx
        pr[1, at, :] = dx * dy
        pr[2, at, :] = dy * dy

    blocks(first, last, gradient_block)

    def kappa_block(r):
        at = pl.ds(r, step)
        above, mid, below = stacked(s[pl.ds(r - 8, step + 16), :])
        up = jnp.sqrt(mid * above)
        down = jnp.sqrt(mid * below)
        left = jnp.sqrt(mid * lane_roll(mid, 1))
        right = lane_roll(left, -1)
        ku[at, :] = up
        kd[at, :] = down
        kl[at, :] = left
        kr[at, :] = right
        ks[at, :] = up + down + left + right + 2.0 * COUPLING

    blocks(16, total - 16, kappa_block)

    @pl.when(has_next)
    def _():
        tile_b.wait_recv()
        fwd_top.wait_recv()
        fwd_bottom.wait_recv()
        fwd_left.wait_recv()
        fwd_right.wait_recv()

    unpack(b, next_left, next_right, 0)

    def change_block(r):
        at = pl.ds(r, step)
        change = b[at, :] - a[at, :]
        pr[3, at, :] = gx[at, :] * change
        pr[4, at, :] = gy[at, :] * change

    blocks(first, last, change_block)

    scale = jnp.where(has_next, jnp.float32(1.0), jnp.float32(0.0))
    cells = float((2 * RADIUS + 1) ** 2)

    def tensor_block(r):
        at = pl.ds(r, step)
        parts = []
        for k in range(5):
            around = pr[k, pl.ds(r - 8, step + 16), :]
            summed = window_sum(around, 0)[8 : 8 + step, :]
            value = window_sum(summed, 1) * (scale / cells)
            tt[k, at, :] = value
            parts.append(value)
        xx, xy, yy, xt, yt = parts
        diag = ks[at, :]
        one, two = xx + diag, yy + diag
        inverse = 1.0 / (one * two - xy * xy)
        va, vb, vc = two * inverse, xy * inverse, one * inverse
        ca[at, :] = va
        cb[at, :] = vb
        cc[at, :] = vc
        f0[0, at, :] = vb * yt - va * xt
        f0[1, at, :] = vb * xt - vc * yt

    blocks(16, total - 16, tensor_block)
    put_tensor = pltpu.make_async_copy(
        tt.at[:, inner, main], tensor_out.at[:, 0], local_sem.at[0]
    )
    put_tensor.start()

    def sweep(source, target, right_x, right_y):
        def body(r):
            at = pl.ds(r, step)
            vu, vd, vl, vr = ku[at, :], kd[at, :], kl[at, :], kr[at, :]

            def near(part):
                up, mid, down = stacked(source[part, pl.ds(r - 8, step + 16), :])
                return (
                    vu * up + vd * down
                    + vl * lane_roll(mid, 1) + vr * lane_roll(mid, -1)
                )

            rx = near(0) + right_x(at)
            ry = near(1) + right_y(at)
            va, vb, vc = ca[at, :], cb[at, :], cc[at, :]
            target[0, at, :] = va * rx - vb * ry
            target[1, at, :] = vc * ry - vb * rx

        blocks(16, total - 16, body)

    for k in range(SWEEPS - 1):
        source, target = (f0, f1) if k % 2 == 0 else (f1, f0)
        sweep(source, target, lambda at: -tt[3, at, :], lambda at: -tt[4, at, :])
    now, other = (f1, f0) if (SWEEPS - 1) % 2 == 1 else (f0, f1)

    span = pl.ds(16, total - 32)
    rim[...] = packed_rim(now, piece, first, width, lane)
    field_next = remote(now.at[:, span, main], main_before, FIELD_NEXT, next_id)
    field_prev = remote(now.at[:, span, main], main_after, FIELD_PREV, prev_id)
    rim_next = remote(rim, rim_before, RIM_NEXT, next_id)
    rim_prev = remote(rim, rim_after, RIM_PREV, prev_id)

    @pl.when(has_next)
    def _():
        rim_next.start()
        field_next.start()

    @pl.when(has_prev)
    def _():
        rim_prev.start()
        field_prev.start()

    @pl.when(has_prev)
    def _():
        rim_next.wait_recv()
        field_next.wait_recv()

    @pl.when(has_next)
    def _():
        rim_prev.wait_recv()
        field_prev.wait_recv()

    both = rim_before[...] + rim_after[...]
    for j in range(FOLD):
        at = pl.ds(first + j * piece, piece)
        for k, ref in enumerate((bx, by)):
            low = (2 * j + k) * SLOT
            head = jnp.where(lane < 8, lane_roll(both, -low), 0.0)
            tail = lane_roll(both, LANES - 16 - low)
            ref[at, pl.ds(width, LANES)] = jnp.where(lane >= LANES - 8, tail, head)

    def beside_block(r):
        at = pl.ds(r, step)
        there = pl.ds(pl.multiple_of(r - 16, 8), step)
        for part, ref in enumerate((bx, by)):
            ref[at, main] = (
                COUPLING * (main_before[part, there, :] + main_after[part, there, :])
                - tt[3 + part, at, main]
            )
            ref[at, pl.ds(width, LANES)] = (
                COUPLING * ref[at, pl.ds(width, LANES)] - tt[3 + part, at, pl.ds(width, LANES)]
            )

    blocks(16, total - 16, beside_block)

    @pl.when(has_next)
    def _():
        field_next.wait_send()
        rim_next.wait_send()

    @pl.when(has_prev)
    def _():
        field_prev.wait_send()
        rim_prev.wait_send()

    for k in range(SWEEPS):
        sweep(now, other, lambda at: bx[at, :], lambda at: by[at, :])
        now, other = other, now

    put_field = pltpu.make_async_copy(
        now.at[:, inner, main], field_out.at[:, 0], local_sem.at[1]
    )
    put_field.start()

    @pl.when(has_up)
    def _():
        a_up.wait_send()
        s_up.wait_send()

    @pl.when(has_down)
    def _():
        a_down.wait_send()
        s_down.wait_send()

    @pl.when(has_right)
    def _():
        col_right.wait_send()

    @pl.when(has_left)
    def _():
        col_left.wait_send()

    @pl.when(has_prev)
    def _():
        for copy in (tile_b, fwd_top, fwd_bottom, fwd_left, fwd_right):
            copy.wait_send()

    put_tensor.wait()
    put_field.wait()


def packed_rim(field, piece, first, width, lane):
    out = jnp.zeros((piece, LANES), jnp.float32)
    for j in range(FOLD):
        at = pl.ds(first + j * piece, piece)
        for k in range(2):
            low = (2 * j + k) * SLOT
            block = field[k, at, pl.ds(width, LANES)]
            head = lane_roll(block, low)
            tail = lane_roll(block, low + SLOT)
            out = jnp.where((lane >= low) & (lane < low + 8), head, out)
            out = jnp.where((lane >= low + 8) & (lane < low + 16), tail, out)
    return out


def local(counts, images, stiffness):
    _, rows, width = images.shape
    total, wide = rows + 2 * EDGE, width + LANES
    piece = (total - 16) // FOLD
    f32 = jnp.float32
    plane = pltpu.VMEM((total, wide), f32)
    packet = pltpu.VMEM((piece, LANES), f32)
    pair = pltpu.VMEM((2, total, wide), f32)
    mains = pltpu.VMEM((2, total - 32, width), f32)
    return pl.pallas_call(
        functools.partial(kernel, counts),
        out_shape=(
            jax.ShapeDtypeStruct((5, 1, rows, width), f32),
            jax.ShapeDtypeStruct((2, 1, rows, width), f32),
        ),
        in_specs=[pl.BlockSpec(memory_space=pl.ANY)] * 2,
        out_specs=[pl.BlockSpec(memory_space=pl.ANY)] * 2,
        scratch_shapes=[plane] * 10
        + [pltpu.VMEM((5, total, wide), f32)] * 2
        + [plane] * 5
        + [pair] * 2
        + [packet] * 9
        + [mains] * 2
        + [
            pltpu.SemaphoreType.DMA((2,)),
            pltpu.SemaphoreType.DMA((COPIES,)),
            pltpu.SemaphoreType.DMA((COPIES,)),
        ],
        compiler_params=pltpu.CompilerParams(
            collective_id=0, has_side_effects=True, vmem_limit_bytes=48 * 1024 * 1024
        ),
    )(images, stiffness)


def solution(mesh):
    counts = tuple(mesh.shape[name] for name in ("sec", "row", "col"))
    spec = P("sec", "row", "col")
    out = P(None, "sec", "row", "col")
    return jax.shard_map(
        functools.partial(local, counts), mesh=mesh, in_specs=(spec, spec),
        out_specs=(out, out), check_vma=False,
    )
```

```python
import functools

import jax
import jax.numpy as jnp
from jax import lax
from jax.experimental import pallas as pl
from jax.experimental.pallas import tpu as pltpu
from jax.sharding import PartitionSpec as P

RADIUS = 4
SWEEPS = 4
ROUNDS = 2
COUPLING = 0.25
MESH = pl.DeviceIdType.MESH

LANES = 128
HALO = 16
EDGE = HALO + 8
SLOT = 16
FOLD = LANES // (2 * SLOT)

(
    TILE_B, ROW_A_UP, ROW_A_DOWN, ROW_S_UP, ROW_S_DOWN, FWD_TOP, FWD_BOTTOM, COL_RIGHT, COL_LEFT,
    FWD_RIGHT, FWD_LEFT, FIELD_NEXT, FIELD_PREV, RIM_NEXT, RIM_PREV,
) = range(15)
KINDS = 15


def lane_roll(x, shift):
    return pltpu.roll(x, shift % x.shape[1], 1)


def shifted(blocks, shift, lane):
    rolled = [lane_roll(x, shift) for x in blocks]
    out = []
    for k, here in enumerate(rolled):
        if shift > 0:
            out.append(jnp.where(lane < shift, rolled[k - 1], here))
        else:
            out.append(jnp.where(lane >= LANES + shift, rolled[(k + 1) % len(rolled)], here))
    return out


def add(*terms):
    return [sum(xs[1:], xs[0]) for xs in zip(*terms)]


def kernel(
    counts, images, stiff, tensor_out, field_out,
    a, b, s, q, gx, gy, pr, p3, tt, ua, ub, uc, va, vb, vc, ex, ey, g0, g1, field,
    send_right, send_left, got_left, got_right, next_left, next_right,
    rim, rim_before, rim_after, main_before, main_after,
    local_sem, send_sem, recv_sem,
):
    sec, row, col = (lax.axis_index(name) for name in ("sec", "row", "col"))
    n_sec, n_row, n_col = counts
    rows, width = images.shape[1], images.shape[2]
    nb, total, _ = a.shape
    nw = nb - 1
    has_prev, has_next = sec > 0, sec < n_sec - 1
    has_up, has_down = row > 0, row < n_row - 1
    has_left, has_right = col > 0, col < n_col - 1
    sides = (
        (has_prev, (sec - 1, row, col)), (has_next, (sec + 1, row, col)),
        (has_up, (sec, row - 1, col)), (has_down, (sec, row + 1, col)),
        (has_left, (sec, row, col - 1)), (has_right, (sec, row, col + 1)),
    )
    prev_id, next_id, up_id, down_id, left_id, right_id = (side[1] for side in sides)
    end = EDGE + rows
    first, last = 8, total - 8
    inner = pl.ds(EDGE, rows)
    main = pl.ds(0, nw)
    top, bottom = pl.ds(EDGE - HALO, HALO), pl.ds(end, HALO)
    piece = (last - first) // FOLD

    def remote(src, dst, k, device, part=0):
        return pltpu.make_async_remote_copy(
            src_ref=src, dst_ref=dst, send_sem=send_sem.at[k, part],
            recv_sem=recv_sem.at[k, part], device_id=device, device_id_type=MESH,
        )

    def columns(k):
        return pl.ds(k * LANES, LANES)

    loads = [
        pltpu.make_async_copy(src.at[0, :, columns(k)], dst.at[k, inner], local_sem.at[i, k])
        for i, (src, dst) in enumerate(((images, a), (stiff, s)))
        for k in range(nw)
    ]
    for copy in loads:
        copy.start()
    barrier = pltpu.get_barrier_semaphore()
    for there, device in sides:
        @pl.when(there)
        def _():
            pl.semaphore_signal(barrier, inc=1, device_id=device, device_id_type=MESH)

    def clear(ref):
        ref[...] = jnp.zeros(ref.shape, jnp.float32)

    @pl.when(jnp.logical_not(has_up))
    def _():
        clear(a.at[main, top])
        clear(s.at[main, top])

    @pl.when(jnp.logical_not(has_down))
    def _():
        clear(a.at[main, bottom])
        clear(s.at[main, bottom])

    @pl.when(jnp.logical_not(has_left))
    def _():
        clear(got_left)

    @pl.when(jnp.logical_not(has_right))
    def _():
        clear(got_right)

    @pl.when(jnp.logical_not(has_next))
    def _():
        clear(b)
        clear(next_left)
        clear(next_right)
        clear(rim_after)
        clear(main_after)

    @pl.when(jnp.logical_not(has_prev))
    def _():
        clear(rim_before)
        clear(main_before)

    for start in (0, total - 8):
        clear(a.at[:, pl.ds(start, 8)])
    for start in (8, total - 16):
        for ref in (g0, g1, field):
            clear(ref.at[:, :, pl.ds(start, 8)])

    pl.semaphore_wait(barrier, sum(jnp.where(there, 1, 0) for there, _device in sides))

    def by_block(src, at, dst, to, k, device):
        return [
            remote(src.at[0, at, columns(p)], dst.at[p, to], k, device, p) for p in range(nw)
        ]

    low, high = pl.ds(0, HALO), pl.ds(rows - HALO, HALO)
    tile_b = by_block(images, pl.ds(0, rows), b, inner, TILE_B, prev_id)
    up = by_block(stiff, low, s, bottom, ROW_S_UP, up_id)
    up += by_block(images, low, a, bottom, ROW_A_UP, up_id)
    down = by_block(stiff, high, s, top, ROW_S_DOWN, down_id)
    down += by_block(images, high, a, top, ROW_A_DOWN, down_id)
    col_right = remote(send_right, got_left, COL_RIGHT, right_id)
    col_left = remote(send_left, got_right, COL_LEFT, left_id)
    forward_rows = [
        remote(a.at[main, top], b.at[main, top], FWD_TOP, prev_id),
        remote(a.at[main, bottom], b.at[main, bottom], FWD_BOTTOM, prev_id),
    ]
    forward_cols = [
        remote(got_left, next_left, FWD_LEFT, prev_id),
        remote(got_right, next_right, FWD_RIGHT, prev_id),
    ]

    def when_start(there, copies):
        @pl.when(there)
        def _():
            for copy in copies:
                copy.start()

    def when_got(there, copies):
        @pl.when(there)
        def _():
            for copy in copies:
                copy.wait_recv()

    def when_sent(there, copies):
        @pl.when(there)
        def _():
            for copy in copies:
                copy.wait_send()

    when_start(has_up, up)
    when_start(has_down, down)
    when_start(has_prev, tile_b)
    for copy in loads:
        copy.wait()
    when_got(has_up, down)
    when_got(has_down, up)
    when_start(has_prev, forward_rows)

    def lanes_of(count):
        return lax.broadcasted_iota(jnp.int32, (count, LANES), 1)

    lane = lanes_of(piece)

    def packed(block, at):
        out = jnp.zeros((piece, LANES), jnp.float32)
        for j in range(FOLD):
            span = pl.ds(first + j * piece, piece)
            for k, ref in enumerate((a, s)):
                low = (2 * j + k) * SLOT
                moved = lane_roll(ref[block, span, :], low - at)
                out = jnp.where((lane >= low) & (lane < low + SLOT), moved, out)
        return out

    def unpack(ref, left, right, k):
        for j in range(FOLD):
            low = (2 * j + k) * SLOT
            from_right = jnp.where(lane < SLOT, lane_roll(right[...], -low), 0.0)
            from_left = lane_roll(left[...], LANES - SLOT - low)
            ref[nw, pl.ds(first + j * piece, piece), :] = jnp.where(
                lane >= LANES - SLOT, from_left, from_right
            )

    @pl.when(has_right)
    def _():
        send_right[...] = packed(nw - 1, LANES - SLOT)
        col_right.start()

    @pl.when(has_left)
    def _():
        send_left[...] = packed(0, 0)
        col_left.start()

    when_got(has_left, [col_right])
    when_got(has_right, [col_left])
    when_start(has_prev, forward_cols)
    unpack(a, got_left, got_right, 0)
    unpack(s, got_left, got_right, 1)

    def blocks(low, high, step, body):
        def one(i, carry):
            body(pl.multiple_of(low + i * step, 8), step)
            return carry

        count = (high - low) // step
        lax.fori_loop(0, count, one, 0)
        rest = high - low - count * step
        if rest:
            body(low + count * step, rest)

    def get(ref, r, step, *lead):
        return [ref[(*lead, k, pl.ds(r, step), slice(None))] for k in range(nb)]

    def put(ref, values, r, step, *lead):
        for k, value in enumerate(values):
            ref[(*lead, k, pl.ds(r, step), slice(None))] = value

    def gradient_block(r, step):
        lane = lanes_of(step)
        rr = lax.broadcasted_iota(jnp.int32, (step, LANES), 0) + r
        row_ok = ((rr >= EDGE) | has_up) & ((rr < end) | has_down)
        rim_ok = ((lane < LANES // 2) & has_right) | ((lane >= LANES // 2) & has_left)
        masks = [row_ok] * nw + [row_ok & rim_ok]
        mid = get(a, r, step)
        after, before = shifted(mid, -1, lane), shifted(mid, 1, lane)
        under, over = get(a, r + 1, step), get(a, r - 1, step)
        dx = [jnp.where(m, (x - y) * 0.5, 0.0) for m, x, y in zip(masks, after, before)]
        dy = [jnp.where(m, (x - y) * 0.5, 0.0) for m, x, y in zip(masks, under, over)]
        put(gx, dx, r, step)
        put(gy, dy, r, step)
        put(pr, [x * x for x in dx], r, step, 0)
        put(pr, [x * y for x, y in zip(dx, dy)], r, step, 1)
        put(pr, [y * y for y in dy], r, step, 2)
        put(q, [jnp.sqrt(x) for x in get(s, r, step)], r, step)

    blocks(first, last, 16, gradient_block)

    def three_rows(k):
        def body(r, step):
            put(p3, add(*(get(pr, r + d, step, k) for d in (-1, 0, 1))), r, step, k)

        return body

    def three_first(r, step):
        for k in range(3):
            three_rows(k)(r, step)

    blocks(first, last, 16, three_first)

    when_got(has_next, tile_b + forward_rows + forward_cols)
    unpack(b, next_left, next_right, 0)

    def change_block(r, step):
        change = [x - y for x, y in zip(get(b, r, step), get(a, r, step))]
        put(pr, [x * y for x, y in zip(get(gx, r, step), change)], r, step, 3)
        put(pr, [x * y for x, y in zip(get(gy, r, step), change)], r, step, 4)

    blocks(first, last, 32, change_block)

    def three_second(r, step):
        for k in (3, 4):
            three_rows(k)(r, step)

    blocks(first, last, 16, three_second)

    scale = jnp.where(has_next, jnp.float32(1.0), jnp.float32(0.0))
    scale = scale * (1.0 / float((2 * RADIUS + 1) ** 2))

    def tensor_block(r, step):
        lane = lanes_of(step)
        parts = []
        for k in range(5):
            summed = add(*(get(p3, r + d, step, k) for d in (-3, 0, 3)))
            summed = add(summed, shifted(summed, 1, lane), shifted(summed, -1, lane))
            summed = add(summed, shifted(summed, 3, lane), shifted(summed, -3, lane))
            parts.append([x * scale for x in summed])
            put(tt, parts[-1], r, step, k)
        mid = get(q, r, step)
        around = add(
            get(q, r - 1, step), get(q, r + 1, step), shifted(mid, 1, lane), shifted(mid, -1, lane)
        )
        for k in range(nb):
            xx, xy, yy, xt, yt = (part[k] for part in parts)
            diag = mid[k] * around[k] + 2.0 * COUPLING
            one, two = xx + diag, yy + diag
            inverse = 1.0 / (one * two - xy * xy)
            ca, cb, cc = two * inverse, xy * inverse, one * inverse
            x, y = cb * yt - ca * xt, cb * xt - cc * yt
            at = pl.ds(r, step)
            for ref, value in ((va, ca), (vb, cb), (vc, cc)):
                ref[k, at, :] = value * COUPLING
            for ref, value in ((ua, ca), (ub, cb), (uc, cc)):
                ref[k, at, :] = value * mid[k]
            ex[k, at, :] = x
            ey[k, at, :] = y
            g0[0, k, at, :] = x * mid[k]
            g0[1, k, at, :] = y * mid[k]

    blocks(16, total - 16, 16, tensor_block)
    put_tensor = [
        pltpu.make_async_copy(
            tt.at[:, k, inner], tensor_out.at[:, 0, :, columns(k)], local_sem.at[0, k]
        )
        for k in range(nw)
    ]
    for copy in put_tensor:
        copy.start()

    def relaxed(source, r, step, x, y):
        lane = lanes_of(step)

        def near(part):
            mid = get(source, r, step, part)
            return add(
                get(source, r - 1, step, part), get(source, r + 1, step, part),
                shifted(mid, 1, lane), shifted(mid, -1, lane),
            )

        nx, ny = near(0), near(1)
        ca, cb, cc = (get(ref, r, step) for ref in (ua, ub, uc))
        return (
            [x[k] + ca[k] * nx[k] - cb[k] * ny[k] for k in range(nb)],
            [y[k] + cc[k] * ny[k] - cb[k] * nx[k] for k in range(nb)],
        )

    def sweep(source, target, final, low, high):
        def body(r, step):
            new = relaxed(source, r, step, get(ex, r, step), get(ey, r, step))
            if not final:
                mid = get(q, r, step)
                new = [[m * x for m, x in zip(mid, part)] for part in new]
            for part in range(2):
                put(target, new[part], r, step, part)

        blocks(low, high, 32, body)

    now, other = g0, g1
    for k in range(1, SWEEPS):
        final = k == SWEEPS - 1
        sweep(now, field if final else other, final, 16, total - 16)
        if not final:
            now, other = other, now

    span = pl.ds(16, total - 32)
    rim[...] = packed_rim(field, piece, first, nw, lane)
    to_next = [
        remote(rim, rim_before, RIM_NEXT, next_id),
        remote(field.at[:, main, span], main_before, FIELD_NEXT, next_id),
    ]
    to_prev = [
        remote(rim, rim_after, RIM_PREV, prev_id),
        remote(field.at[:, main, span], main_after, FIELD_PREV, prev_id),
    ]
    when_start(has_next, to_next)
    when_start(has_prev, to_prev)
    def scale_block(r, step):
        mid = get(q, r, step)
        for part in range(2):
            put(g0, [m * x for m, x in zip(mid, get(field, r, step, part))], r, step, part)

    blocks(16, total - 16, 32, scale_block)
    when_got(has_prev, to_next)
    when_got(has_next, to_prev)

    both = rim_before[...] + rim_after[...]
    for j in range(FOLD):
        for k, ref in enumerate((gx, gy)):
            low = (2 * j + k) * SLOT
            head = jnp.where(lane < 8, lane_roll(both, -low), 0.0)
            tail = lane_roll(both, LANES - 16 - low)
            ref[nw, pl.ds(first + j * piece, piece), :] = jnp.where(lane >= LANES - 8, tail, head)

    def first_block(r, step):
        there = pl.ds(r - 16, step)
        at = pl.ds(r, step)

        def beside(part, ref):
            return [
                main_before[part, k, there, :] + main_after[part, k, there, :] for k in range(nw)
            ] + [ref[nw, at, :]]

        x, y = beside(0, gx), beside(1, gy)
        ca, cb, cc = (get(ref, r, step) for ref in (va, vb, vc))
        old_x, old_y = get(ex, r, step), get(ey, r, step)
        new_x = [old_x[k] + ca[k] * x[k] - cb[k] * y[k] for k in range(nb)]
        new_y = [old_y[k] + cc[k] * y[k] - cb[k] * x[k] for k in range(nb)]
        put(ex, new_x, r, step)
        put(ey, new_y, r, step)
        mid = get(q, r, step)
        for part, values in enumerate(relaxed(g0, r, step, new_x, new_y)):
            put(g1, [m * v for m, v in zip(mid, values)], r, step, part)

    blocks(16, total - 16, 16, first_block)
    when_sent(has_next, to_next)
    when_sent(has_prev, to_prev)
    now, other = g1, g0
    for k in range(1, SWEEPS):
        final = k == SWEEPS - 1
        if final:
            sweep(now, field, final, EDGE, end)
        else:
            sweep(now, other, final, 16, total - 16)
        now, other = other, now

    put_field = [
        pltpu.make_async_copy(
            field.at[:, k, inner], field_out.at[:, 0, :, columns(k)], local_sem.at[1, k]
        )
        for k in range(nw)
    ]
    for copy in put_field:
        copy.start()
    when_sent(has_up, up)
    when_sent(has_down, down)
    when_sent(has_right, [col_right])
    when_sent(has_left, [col_left])
    when_sent(has_prev, tile_b + forward_rows + forward_cols)
    for copy in put_tensor + put_field:
        copy.wait()


def packed_rim(field, piece, first, nw, lane):
    out = jnp.zeros((piece, LANES), jnp.float32)
    for j in range(FOLD):
        at = pl.ds(first + j * piece, piece)
        for k in range(2):
            low = (2 * j + k) * SLOT
            block = field[k, nw, at, :]
            head = lane_roll(block, low)
            tail = lane_roll(block, low + SLOT)
            out = jnp.where((lane >= low) & (lane < low + 8), head, out)
            out = jnp.where((lane >= low + 8) & (lane < low + 16), tail, out)
    return out


def local(counts, images, stiffness):
    _, rows, width = images.shape
    nw = width // LANES
    nb = nw + 1
    total = rows + 2 * EDGE
    f32 = jnp.float32
    plane = pltpu.VMEM((nb, total, LANES), f32)
    five = pltpu.VMEM((5, nb, total, LANES), f32)
    pair = pltpu.VMEM((2, nb, total, LANES), f32)
    packet = pltpu.VMEM(((total - 16) // FOLD, LANES), f32)
    mains = pltpu.VMEM((2, nw, total - 32, LANES), f32)
    return pl.pallas_call(
        functools.partial(kernel, counts),
        out_shape=(
            jax.ShapeDtypeStruct((5, 1, rows, width), f32),
            jax.ShapeDtypeStruct((2, 1, rows, width), f32),
        ),
        in_specs=[pl.BlockSpec(memory_space=pltpu.HBM)] * 2,
        out_specs=[pl.BlockSpec(memory_space=pl.ANY)] * 2,
        scratch_shapes=[plane] * 6
        + [five] * 3
        + [plane] * 8
        + [pair] * 3
        + [packet] * 9
        + [mains] * 2
        + [
            pltpu.SemaphoreType.DMA((2, nw)),
            pltpu.SemaphoreType.DMA((KINDS, nw)),
            pltpu.SemaphoreType.DMA((KINDS, nw)),
        ],
        compiler_params=pltpu.CompilerParams(
            collective_id=0, has_side_effects=True, vmem_limit_bytes=48 * 1024 * 1024
        ),
    )(images, stiffness)


def solution(mesh):
    counts = tuple(mesh.shape[name] for name in ("sec", "row", "col"))
    spec = P("sec", "row", "col")
    out = P(None, "sec", "row", "col")
    return jax.shard_map(
        functools.partial(local, counts), mesh=mesh, in_specs=(spec, spec),
        out_specs=(out, out), check_vma=False,
    )
```

```python
import functools

import jax
import jax.numpy as jnp
from jax import lax
from jax.experimental import pallas as pl
from jax.experimental.pallas import tpu as pltpu
from jax.sharding import PartitionSpec as P

RADIUS = 4
SWEEPS = 4
ROUNDS = 2
COUPLING = 0.25
MESH = pl.DeviceIdType.MESH

LANES = 128
HALO = 16
EDGE = HALO + 8
SLOT = 16
CHUNK = 96
FOLD = LANES // (2 * SLOT)

(
    TILE_B, ROW_A_UP, ROW_A_DOWN, ROW_S_UP, ROW_S_DOWN, FWD_TOP, FWD_BOTTOM, COL_RIGHT, COL_LEFT,
    FWD_RIGHT, FWD_LEFT,
) = range(11)
KINDS = 11


def lane_roll(x, shift):
    return pltpu.roll(x, shift % x.shape[1], 1)


def shifted(blocks, shift, lane):
    rolled = [lane_roll(x, shift) for x in blocks]
    out = []
    for k, here in enumerate(rolled):
        if shift > 0:
            out.append(jnp.where(lane < shift, rolled[k - 1], here))
        else:
            out.append(jnp.where(lane >= LANES + shift, rolled[(k + 1) % len(rolled)], here))
    return out


def add(*terms):
    return [sum(xs[1:], xs[0]) for xs in zip(*terms)]


def kernel(
    counts, images, stiff, tensor_out, field_out,
    a, b, s, q, gx, gy, pr, p3, tt, ua, ub, uc, va, vb, vc, ex, ey, g0, g1, field, last_field,
    send_right, send_left, got_left, got_right, next_left, next_right,
    rim, rim_before, rim_after, main_before, main_after,
    local_sem, send_sem, recv_sem, chunk_send, chunk_recv,
):
    sec, row, col = (lax.axis_index(name) for name in ("sec", "row", "col"))
    n_sec, n_row, n_col = counts
    rows, width = images.shape[1], images.shape[2]
    nb, total, _ = a.shape
    nw = nb - 1
    has_prev, has_next = sec > 0, sec < n_sec - 1
    has_up, has_down = row > 0, row < n_row - 1
    has_left, has_right = col > 0, col < n_col - 1
    sides = (
        (has_prev, (sec - 1, row, col)), (has_next, (sec + 1, row, col)),
        (has_up, (sec, row - 1, col)), (has_down, (sec, row + 1, col)),
        (has_left, (sec, row, col - 1)), (has_right, (sec, row, col + 1)),
    )
    prev_id, next_id, up_id, down_id, left_id, right_id = (side[1] for side in sides)
    end = EDGE + rows
    first, last = 8, total - 8
    inner = pl.ds(EDGE, rows)
    main = pl.ds(0, nw)
    top, bottom = pl.ds(EDGE - HALO, HALO), pl.ds(end, HALO)
    piece = (last - first) // FOLD

    def remote(src, dst, k, device, part=0):
        return pltpu.make_async_remote_copy(
            src_ref=src, dst_ref=dst, send_sem=send_sem.at[k, part],
            recv_sem=recv_sem.at[k, part], device_id=device, device_id_type=MESH,
        )

    def columns(k):
        return pl.ds(k * LANES, LANES)

    loads = [
        pltpu.make_async_copy(src.at[0, :, columns(k)], dst.at[k, inner], local_sem.at[i, k])
        for i, (src, dst) in enumerate(((images, a), (stiff, s)))
        for k in range(nw)
    ]
    for copy in loads:
        copy.start()
    barrier = pltpu.get_barrier_semaphore()
    for there, device in sides:
        @pl.when(there)
        def _():
            pl.semaphore_signal(barrier, inc=1, device_id=device, device_id_type=MESH)

    def clear(ref):
        ref[...] = jnp.zeros(ref.shape, jnp.float32)

    @pl.when(jnp.logical_not(has_up))
    def _():
        clear(a.at[main, top])
        clear(s.at[main, top])

    @pl.when(jnp.logical_not(has_down))
    def _():
        clear(a.at[main, bottom])
        clear(s.at[main, bottom])

    @pl.when(jnp.logical_not(has_left))
    def _():
        clear(got_left)

    @pl.when(jnp.logical_not(has_right))
    def _():
        clear(got_right)

    @pl.when(jnp.logical_not(has_next))
    def _():
        clear(b)
        clear(next_left)
        clear(next_right)
        clear(rim_after)
        clear(main_after)

    @pl.when(jnp.logical_not(has_prev))
    def _():
        clear(rim_before)
        clear(main_before)

    for start in (0, total - 8):
        for ref in (a, q):
            clear(ref.at[:, pl.ds(start, 8)])
        for ref in (pr, p3, g0, g1):
            clear(ref.at[:, :, pl.ds(start, 8)])
    for start in (8, total - 16):
        for ref in (main_before, main_after):
            clear(ref.at[:, :, pl.ds(start, 8)])

    pl.semaphore_wait(barrier, sum(jnp.where(there, 1, 0) for there, _device in sides))

    def by_block(src, at, dst, to, k, device):
        return [
            remote(src.at[0, at, columns(p)], dst.at[p, to], k, device, p) for p in range(nw)
        ]

    low, high = pl.ds(0, HALO), pl.ds(rows - HALO, HALO)
    tile_b = by_block(images, pl.ds(0, rows), b, inner, TILE_B, prev_id)
    up = by_block(stiff, low, s, bottom, ROW_S_UP, up_id)
    up += by_block(images, low, a, bottom, ROW_A_UP, up_id)
    down = by_block(stiff, high, s, top, ROW_S_DOWN, down_id)
    down += by_block(images, high, a, top, ROW_A_DOWN, down_id)
    col_right = remote(send_right, got_left, COL_RIGHT, right_id)
    col_left = remote(send_left, got_right, COL_LEFT, left_id)
    forward_rows = [
        remote(a.at[main, top], b.at[main, top], FWD_TOP, prev_id),
        remote(a.at[main, bottom], b.at[main, bottom], FWD_BOTTOM, prev_id),
    ]
    forward_cols = [
        remote(got_left, next_left, FWD_LEFT, prev_id),
        remote(got_right, next_right, FWD_RIGHT, prev_id),
    ]

    def when_start(there, copies):
        @pl.when(there)
        def _():
            for copy in copies:
                copy.start()

    def when_got(there, copies):
        @pl.when(there)
        def _():
            for copy in copies:
                copy.wait_recv()

    def when_sent(there, copies):
        @pl.when(there)
        def _():
            for copy in copies:
                copy.wait_send()

    when_start(has_up, up)
    when_start(has_down, down)
    when_start(has_prev, tile_b)
    for copy in loads:
        copy.wait()
    when_got(has_up, down)
    when_got(has_down, up)
    when_start(has_prev, forward_rows)

    def lanes_of(count):
        return lax.broadcasted_iota(jnp.int32, (count, LANES), 1)

    lane = lanes_of(piece)

    def packed(block, at):
        out = jnp.zeros((piece, LANES), jnp.float32)
        for j in range(FOLD):
            span = pl.ds(first + j * piece, piece)
            for k, ref in enumerate((a, s)):
                low = (2 * j + k) * SLOT
                moved = lane_roll(ref[block, span, :], low - at)
                out = jnp.where((lane >= low) & (lane < low + SLOT), moved, out)
        return out

    def unpack(ref, left, right, k):
        for j in range(FOLD):
            low = (2 * j + k) * SLOT
            from_right = jnp.where(lane < SLOT, lane_roll(right[...], -low), 0.0)
            from_left = lane_roll(left[...], LANES - SLOT - low)
            ref[nw, pl.ds(first + j * piece, piece), :] = jnp.where(
                lane >= LANES - SLOT, from_left, from_right
            )

    @pl.when(has_right)
    def _():
        send_right[...] = packed(nw - 1, LANES - SLOT)
        col_right.start()

    @pl.when(has_left)
    def _():
        send_left[...] = packed(0, 0)
        col_left.start()

    when_got(has_left, [col_right])
    when_got(has_right, [col_left])
    when_start(has_prev, forward_cols)
    unpack(a, got_left, got_right, 0)
    unpack(s, got_left, got_right, 1)

    def blocks(low, high, step, body):
        def one(i, carry):
            body(pl.multiple_of(low + i * step, 8), step)
            return carry

        count = (high - low) // step
        lax.fori_loop(0, count, one, 0)
        rest = high - low - count * step
        if rest:
            body(low + count * step, rest)

    def get(ref, r, step, *lead):
        return [ref[(*lead, k, pl.ds(r, step), slice(None))] for k in range(nb)]

    def put(ref, values, r, step, *lead):
        for k, value in enumerate(values):
            ref[(*lead, k, pl.ds(r, step), slice(None))] = value

    def gradient_block(r, step):
        lane = lanes_of(step)
        rr = lax.broadcasted_iota(jnp.int32, (step, LANES), 0) + r
        row_ok = ((rr >= EDGE) | has_up) & ((rr < end) | has_down)
        rim_ok = ((lane < LANES // 2) & has_right) | ((lane >= LANES // 2) & has_left)
        masks = [row_ok] * nw + [row_ok & rim_ok]
        mid = get(a, r, step)
        after, before = shifted(mid, -1, lane), shifted(mid, 1, lane)
        under, over = get(a, r + 1, step), get(a, r - 1, step)
        dx = [jnp.where(m, (x - y) * 0.5, 0.0) for m, x, y in zip(masks, after, before)]
        dy = [jnp.where(m, (x - y) * 0.5, 0.0) for m, x, y in zip(masks, under, over)]
        put(gx, dx, r, step)
        put(gy, dy, r, step)
        put(pr, [x * x for x in dx], r, step, 0)
        put(pr, [x * y for x, y in zip(dx, dy)], r, step, 1)
        put(pr, [y * y for y in dy], r, step, 2)
        put(q, [jnp.sqrt(x) for x in get(s, r, step)], r, step)

    blocks(first, last, 16, gradient_block)

    def three_rows(k):
        def body(r, step):
            put(p3, add(*(get(pr, r + d, step, k) for d in (-1, 0, 1))), r, step, k)

        return body

    scale = jnp.where(has_next, jnp.float32(1.0), jnp.float32(0.0))
    scale = scale * (1.0 / float((2 * RADIUS + 1) ** 2))

    def window_mean(k, r, step):
        lane = lanes_of(step)
        summed = add(*(get(p3, r + d, step, k) for d in (-3, 0, 3)))
        summed = add(summed, shifted(summed, 1, lane), shifted(summed, -1, lane))
        summed = add(summed, shifted(summed, 3, lane), shifted(summed, -3, lane))
        value = [x * scale for x in summed]
        put(tt, value, r, step, k)
        return value

    def three_first(r, step):
        for k in range(3):
            three_rows(k)(r, step)

    blocks(first, last, 16, three_first)

    def mean_first(r, step):
        for k in range(3):
            window_mean(k, r, step)

    blocks(first, last, 16, mean_first)

    when_got(has_next, tile_b + forward_rows + forward_cols)
    unpack(b, next_left, next_right, 0)

    def change_block(r, step):
        change = [x - y for x, y in zip(get(b, r, step), get(a, r, step))]
        put(pr, [x * y for x, y in zip(get(gx, r, step), change)], r, step, 3)
        put(pr, [x * y for x, y in zip(get(gy, r, step), change)], r, step, 4)

    blocks(first, last, 32, change_block)

    def three_second(r, step):
        for k in (3, 4):
            three_rows(k)(r, step)

    blocks(first, last, 16, three_second)

    def tensor_block(r, step):
        lane = lanes_of(step)
        parts = [get(tt, r, step, k) for k in range(3)]
        parts += [window_mean(k, r, step) for k in (3, 4)]
        mid = get(q, r, step)
        around = add(
            get(q, r - 1, step), get(q, r + 1, step), shifted(mid, 1, lane), shifted(mid, -1, lane)
        )
        for k in range(nb):
            xx, xy, yy, xt, yt = (part[k] for part in parts)
            diag = mid[k] * around[k] + 2.0 * COUPLING
            one, two = xx + diag, yy + diag
            inverse = 1.0 / (one * two - xy * xy)
            ca, cb, cc = two * inverse, xy * inverse, one * inverse
            x, y = cb * yt - ca * xt, cb * xt - cc * yt
            at = pl.ds(r, step)
            for ref, value in ((va, ca), (vb, cb), (vc, cc)):
                ref[k, at, :] = value * COUPLING
            for ref, value in ((ua, ca), (ub, cb), (uc, cc)):
                ref[k, at, :] = value * mid[k]
            ex[k, at, :] = x
            ey[k, at, :] = y
            g0[0, k, at, :] = x * mid[k]
            g0[1, k, at, :] = y * mid[k]

    def relaxed(source, r, step, x, y):
        lane = lanes_of(step)

        def near(part):
            mid = get(source, r, step, part)
            return add(
                get(source, r - 1, step, part), get(source, r + 1, step, part),
                shifted(mid, 1, lane), shifted(mid, -1, lane),
            )

        nx, ny = near(0), near(1)
        ca, cb, cc = (get(ref, r, step) for ref in (ua, ub, uc))
        return (
            [x[k] + ca[k] * nx[k] - cb[k] * ny[k] for k in range(nb)],
            [y[k] + cc[k] * ny[k] - cb[k] * nx[k] for k in range(nb)],
        )

    def sweep(source, target, scaled=None):
        def body(r, step):
            new = relaxed(source, r, step, get(ex, r, step), get(ey, r, step))
            mid = get(q, r, step) if scaled is not None else None
            for part in range(2):
                if target is not None:
                    put(target, new[part], r, step, part)
                if scaled is not None:
                    put(scaled, [m * x for m, x in zip(mid, new[part])], r, step, part)

        return body

    bounds = list(range(first, last - CHUNK + 1, CHUNK)) + [last]
    chunks = len(bounds) - 1

    def stages(c, bodies, lead):
        for k, body in enumerate(bodies):
            ahead = 8 * (lead - k)
            low = first if c == 0 else bounds[c] + ahead
            high = last if c == chunks - 1 else bounds[c + 1] + ahead
            blocks(low, high, 24, body)

    first_round = [tensor_block]
    now, other = g0, g1
    for k in range(1, SWEEPS):
        first_round.append(sweep(now, field if k == SWEEPS - 1 else None, other))
        now, other = other, now

    to_next, to_prev = [], []
    for c in range(chunks):
        stages(c, first_round, SWEEPS - 1)
        low, high = bounds[c], bounds[c + 1]
        folded = pl.ds((low - first) // FOLD, (high - low) // FOLD)
        pack_rim(field, rim, low, high, first, nw)
        rows_sent = pl.ds(max(low, 16), min(high, total - 16) - max(low, 16))

        def moves(rims, mains, device, way):
            pairs = (
                (rim.at[folded], rims.at[folded]),
                (field.at[:, main, rows_sent], mains.at[:, main, rows_sent]),
            )
            return [
                pltpu.make_async_remote_copy(
                    src_ref=src, dst_ref=dst, send_sem=chunk_send.at[way + i, c],
                    recv_sem=chunk_recv.at[way + i, c], device_id=device, device_id_type=MESH,
                )
                for i, (src, dst) in enumerate(pairs)
            ]

        to_next.append(moves(rim_before, main_before, next_id, 0))
        to_prev.append(moves(rim_after, main_after, prev_id, 2))
        when_start(has_next, to_next[c])
        when_start(has_prev, to_prev[c])

    put_tensor = [
        pltpu.make_async_copy(
            tt.at[:, k, inner], tensor_out.at[:, 0, :, columns(k)], local_sem.at[0, k]
        )
        for k in range(nw)
    ]
    for copy in put_tensor:
        copy.start()


    def first_block(r, step):
        at = pl.ds(r, step)

        def beside(part, ref):
            return [
                main_before[part, k, at, :] + main_after[part, k, at, :] for k in range(nw)
            ] + [ref[nw, at, :]]

        x, y = beside(0, gx), beside(1, gy)
        ca, cb, cc = (get(ref, r, step) for ref in (va, vb, vc))
        old_x, old_y = get(ex, r, step), get(ey, r, step)
        new_x = [old_x[k] + ca[k] * x[k] - cb[k] * y[k] for k in range(nb)]
        new_y = [old_y[k] + cc[k] * y[k] - cb[k] * x[k] for k in range(nb)]
        put(ex, new_x, r, step)
        put(ey, new_y, r, step)
        mid = get(q, r, step)
        for part, values in enumerate(relaxed(now, r, step, new_x, new_y)):
            put(other, [m * v for m, v in zip(mid, values)], r, step, part)

    second_round = [first_block]
    source, target = other, now
    for k in range(1, SWEEPS):
        if k == SWEEPS - 1:
            second_round.append(sweep(source, last_field))
        else:
            second_round.append(sweep(source, None, target))
        source, target = target, source

    for c in range(chunks):
        when_got(has_prev, to_next[c])
        when_got(has_next, to_prev[c])
        low, high = bounds[c], bounds[c + 1]
        size = (high - low) // FOLD
        folded = pl.ds((low - first) // FOLD, size)
        both = rim_before[folded, :] + rim_after[folded, :]
        lane = lanes_of(size)
        for j in range(FOLD):
            for k, ref in enumerate((gx, gy)):
                slot = (2 * j + k) * SLOT
                head = jnp.where(lane < 8, lane_roll(both, -slot), 0.0)
                tail = lane_roll(both, LANES - 16 - slot)
                ref[nw, pl.ds(low + j * size, size), :] = jnp.where(
                    lane >= LANES - 8, tail, head
                )
        stages(c, second_round, 0)

    for c in range(chunks):
        when_sent(has_next, to_next[c])
        when_sent(has_prev, to_prev[c])

    put_field = [
        pltpu.make_async_copy(
            last_field.at[:, k, inner], field_out.at[:, 0, :, columns(k)], local_sem.at[1, k]
        )
        for k in range(nw)
    ]
    for copy in put_field:
        copy.start()
    when_sent(has_up, up)
    when_sent(has_down, down)
    when_sent(has_right, [col_right])
    when_sent(has_left, [col_left])
    when_sent(has_prev, tile_b + forward_rows + forward_cols)
    for copy in put_tensor + put_field:
        copy.wait()


def pack_rim(field, rim, low, high, first, nw):
    size = (high - low) // FOLD
    lane = lax.broadcasted_iota(jnp.int32, (size, LANES), 1)
    out = jnp.zeros((size, LANES), jnp.float32)
    for j in range(FOLD):
        at = pl.ds(low + j * size, size)
        for k in range(2):
            slot = (2 * j + k) * SLOT
            block = field[k, nw, at, :]
            head, tail = lane_roll(block, slot), lane_roll(block, slot + SLOT)
            out = jnp.where((lane >= slot) & (lane < slot + 8), head, out)
            out = jnp.where((lane >= slot + 8) & (lane < slot + 16), tail, out)
    rim[pl.ds((low - first) // FOLD, size), :] = out


def local(counts, images, stiffness):
    _, rows, width = images.shape
    nw = width // LANES
    nb = nw + 1
    total = rows + 2 * EDGE
    f32 = jnp.float32
    plane = pltpu.VMEM((nb, total, LANES), f32)
    five = pltpu.VMEM((5, nb, total, LANES), f32)
    pair = pltpu.VMEM((2, nb, total, LANES), f32)
    packet = pltpu.VMEM(((total - 16) // FOLD, LANES), f32)
    mains = pltpu.VMEM((2, nw, total, LANES), f32)
    chunks = (total - 16) // CHUNK
    return pl.pallas_call(
        functools.partial(kernel, counts),
        out_shape=(
            jax.ShapeDtypeStruct((5, 1, rows, width), f32),
            jax.ShapeDtypeStruct((2, 1, rows, width), f32),
        ),
        in_specs=[pl.BlockSpec(memory_space=pltpu.HBM)] * 2,
        out_specs=[pl.BlockSpec(memory_space=pl.ANY)] * 2,
        scratch_shapes=[plane] * 6
        + [five] * 3
        + [plane] * 8
        + [pair] * 4
        + [packet] * 9
        + [mains] * 2
        + [
            pltpu.SemaphoreType.DMA((2, nw)),
            pltpu.SemaphoreType.DMA((KINDS, nw)),
            pltpu.SemaphoreType.DMA((KINDS, nw)),
            pltpu.SemaphoreType.DMA((4, chunks)),
            pltpu.SemaphoreType.DMA((4, chunks)),
        ],
        compiler_params=pltpu.CompilerParams(
            collective_id=0, has_side_effects=True, vmem_limit_bytes=48 * 1024 * 1024
        ),
    )(images, stiffness)


def solution(mesh):
    counts = tuple(mesh.shape[name] for name in ("sec", "row", "col"))
    spec = P("sec", "row", "col")
    out = P(None, "sec", "row", "col")
    return jax.shard_map(
        functools.partial(local, counts), mesh=mesh, in_specs=(spec, spec),
        out_specs=(out, out), check_vma=False,
    )
```

```python
import functools

import jax
import jax.numpy as jnp
from jax import lax
from jax.experimental import pallas as pl
from jax.experimental.pallas import tpu as pltpu
from jax.sharding import PartitionSpec as P

RADIUS = 4
SWEEPS = 4
ROUNDS = 2
COUPLING = 0.25
MESH = pl.DeviceIdType.MESH

LANES = 128
HALO = 16
EDGE = HALO + 8
SLOT = 16
CHUNK = 96
FOLD = LANES // (2 * SLOT)

(
    TILE_B, ROW_A_UP, ROW_A_DOWN, ROW_S_UP, ROW_S_DOWN, FWD_TOP, FWD_BOTTOM, COL_RIGHT, COL_LEFT,
    FWD_RIGHT, FWD_LEFT,
) = range(11)
KINDS = 11


def lane_roll(x, shift):
    return pltpu.roll(x, shift % x.shape[1], 1)


def shifted(blocks, shift, lane):
    rolled = [lane_roll(x, shift) for x in blocks]
    out = []
    for k, here in enumerate(rolled):
        if shift > 0:
            out.append(jnp.where(lane < shift, rolled[k - 1], here))
        else:
            out.append(jnp.where(lane >= LANES + shift, rolled[(k + 1) % len(rolled)], here))
    return out


def add(*terms):
    return [sum(xs[1:], xs[0]) for xs in zip(*terms)]


def kernel(
    counts, images, stiff, tensor_out, field_out,
    a, b, s, q, gx, gy, pr, p3, tt, ua, ub, uc, va, vb, vc, ex, ey, g0, g1, field, last_field,
    send_right, send_left, got_left, got_right, next_left, next_right,
    rim, rim_before, rim_after, main_before, main_after,
    local_sem, send_sem, recv_sem, chunk_send, chunk_recv,
):
    sec, row, col = (lax.axis_index(name) for name in ("sec", "row", "col"))
    n_sec, n_row, n_col = counts
    rows, width = images.shape[1], images.shape[2]
    nb, total, _ = a.shape
    nw = nb - 1
    has_prev, has_next = sec > 0, sec < n_sec - 1
    has_up, has_down = row > 0, row < n_row - 1
    has_left, has_right = col > 0, col < n_col - 1
    sides = (
        (has_prev, (sec - 1, row, col)), (has_next, (sec + 1, row, col)),
        (has_up, (sec, row - 1, col)), (has_down, (sec, row + 1, col)),
        (has_left, (sec, row, col - 1)), (has_right, (sec, row, col + 1)),
    )
    prev_id, next_id, up_id, down_id, left_id, right_id = (side[1] for side in sides)
    end = EDGE + rows
    first, last = 8, total - 8
    inner = pl.ds(EDGE, rows)
    main = pl.ds(0, nw)
    top, bottom = pl.ds(EDGE - HALO, HALO), pl.ds(end, HALO)
    piece = (last - first) // FOLD

    def remote(src, dst, k, device, part=0):
        return pltpu.make_async_remote_copy(
            src_ref=src, dst_ref=dst, send_sem=send_sem.at[k, part],
            recv_sem=recv_sem.at[k, part], device_id=device, device_id_type=MESH,
        )

    def columns(k):
        return pl.ds(k * LANES, LANES)

    loads = [
        pltpu.make_async_copy(src.at[0, :, columns(k)], dst.at[k, inner], local_sem.at[i, k])
        for i, (src, dst) in enumerate(((images, a), (stiff, s)))
        for k in range(nw)
    ]
    for copy in loads:
        copy.start()
    barrier = pltpu.get_barrier_semaphore()
    for there, device in sides:
        @pl.when(there)
        def _():
            pl.semaphore_signal(barrier, inc=1, device_id=device, device_id_type=MESH)

    def clear(ref):
        ref[...] = jnp.zeros(ref.shape, jnp.float32)

    @pl.when(jnp.logical_not(has_up))
    def _():
        clear(a.at[main, top])
        clear(s.at[main, top])

    @pl.when(jnp.logical_not(has_down))
    def _():
        clear(a.at[main, bottom])
        clear(s.at[main, bottom])

    @pl.when(jnp.logical_not(has_left))
    def _():
        clear(got_left)

    @pl.when(jnp.logical_not(has_right))
    def _():
        clear(got_right)

    @pl.when(jnp.logical_not(has_next))
    def _():
        clear(b)
        clear(next_left)
        clear(next_right)
        clear(rim_after)
        clear(main_after)

    @pl.when(jnp.logical_not(has_prev))
    def _():
        clear(rim_before)
        clear(main_before)

    for start in (0, total - 8):
        for ref in (a, q):
            clear(ref.at[:, pl.ds(start, 8)])
        for ref in (pr, p3):
            clear(ref.at[:, :, pl.ds(start, 8)])
    for start in (8, total - 16):
        for ref in (g0, g1, field):
            clear(ref.at[:, :, pl.ds(start, 8)])

    pl.semaphore_wait(barrier, sum(jnp.where(there, 1, 0) for there, _device in sides))

    def by_block(src, at, dst, to, k, device):
        return [
            remote(src.at[0, at, columns(p)], dst.at[p, to], k, device, p) for p in range(nw)
        ]

    low, high = pl.ds(0, HALO), pl.ds(rows - HALO, HALO)
    tile_b = by_block(images, pl.ds(0, rows), b, inner, TILE_B, prev_id)
    up = by_block(stiff, low, s, bottom, ROW_S_UP, up_id)
    up += by_block(images, low, a, bottom, ROW_A_UP, up_id)
    down = by_block(stiff, high, s, top, ROW_S_DOWN, down_id)
    down += by_block(images, high, a, top, ROW_A_DOWN, down_id)
    col_right = remote(send_right, got_left, COL_RIGHT, right_id)
    col_left = remote(send_left, got_right, COL_LEFT, left_id)
    forward_rows = [
        remote(a.at[main, top], b.at[main, top], FWD_TOP, prev_id),
        remote(a.at[main, bottom], b.at[main, bottom], FWD_BOTTOM, prev_id),
    ]
    forward_cols = [
        remote(got_left, next_left, FWD_LEFT, prev_id),
        remote(got_right, next_right, FWD_RIGHT, prev_id),
    ]

    def when_start(there, copies):
        @pl.when(there)
        def _():
            for copy in copies:
                copy.start()

    def when_got(there, copies):
        @pl.when(there)
        def _():
            for copy in copies:
                copy.wait_recv()

    def when_sent(there, copies):
        @pl.when(there)
        def _():
            for copy in copies:
                copy.wait_send()

    when_start(has_up, up)
    when_start(has_down, down)
    when_start(has_prev, tile_b)
    for copy in loads:
        copy.wait()
    when_got(has_up, down)
    when_got(has_down, up)
    when_start(has_prev, forward_rows)

    def lanes_of(count):
        return lax.broadcasted_iota(jnp.int32, (count, LANES), 1)

    lane = lanes_of(piece)

    def packed(block, at):
        out = jnp.zeros((piece, LANES), jnp.float32)
        for j in range(FOLD):
            span = pl.ds(first + j * piece, piece)
            for k, ref in enumerate((a, s)):
                low = (2 * j + k) * SLOT
                moved = lane_roll(ref[block, span, :], low - at)
                out = jnp.where((lane >= low) & (lane < low + SLOT), moved, out)
        return out

    def unpack(ref, left, right, k):
        for j in range(FOLD):
            low = (2 * j + k) * SLOT
            from_right = jnp.where(lane < SLOT, lane_roll(right[...], -low), 0.0)
            from_left = lane_roll(left[...], LANES - SLOT - low)
            ref[nw, pl.ds(first + j * piece, piece), :] = jnp.where(
                lane >= LANES - SLOT, from_left, from_right
            )

    @pl.when(has_right)
    def _():
        send_right[...] = packed(nw - 1, LANES - SLOT)
        col_right.start()

    @pl.when(has_left)
    def _():
        send_left[...] = packed(0, 0)
        col_left.start()

    when_got(has_left, [col_right])
    when_got(has_right, [col_left])
    when_start(has_prev, forward_cols)
    unpack(a, got_left, got_right, 0)
    unpack(s, got_left, got_right, 1)

    def blocks(low, high, step, body):
        def one(i, carry):
            body(pl.multiple_of(low + i * step, 8), step)
            return carry

        count = (high - low) // step
        lax.fori_loop(0, count, one, 0)
        rest = high - low - count * step
        if rest:
            body(low + count * step, rest)

    def get(ref, r, step, *lead):
        return [ref[(*lead, k, pl.ds(r, step), slice(None))] for k in range(nb)]

    def put(ref, values, r, step, *lead):
        for k, value in enumerate(values):
            ref[(*lead, k, pl.ds(r, step), slice(None))] = value

    def gradient_block(r, step):
        lane = lanes_of(step)
        rr = lax.broadcasted_iota(jnp.int32, (step, LANES), 0) + r
        row_ok = ((rr >= EDGE) | has_up) & ((rr < end) | has_down)
        rim_ok = ((lane < LANES // 2) & has_right) | ((lane >= LANES // 2) & has_left)
        masks = [row_ok] * nw + [row_ok & rim_ok]
        mid = get(a, r, step)
        after, before = shifted(mid, -1, lane), shifted(mid, 1, lane)
        under, over = get(a, r + 1, step), get(a, r - 1, step)
        dx = [jnp.where(m, (x - y) * 0.5, 0.0) for m, x, y in zip(masks, after, before)]
        dy = [jnp.where(m, (x - y) * 0.5, 0.0) for m, x, y in zip(masks, under, over)]
        put(gx, dx, r, step)
        put(gy, dy, r, step)
        put(pr, [x * x for x in dx], r, step, 0)
        put(pr, [x * y for x, y in zip(dx, dy)], r, step, 1)
        put(pr, [y * y for y in dy], r, step, 2)
        put(q, [jnp.sqrt(x) for x in get(s, r, step)], r, step)

    blocks(first, last, 16, gradient_block)

    def three_rows(k):
        def body(r, step):
            put(p3, add(*(get(pr, r + d, step, k) for d in (-1, 0, 1))), r, step, k)

        return body

    scale = jnp.where(has_next, jnp.float32(1.0), jnp.float32(0.0))
    scale = scale * (1.0 / float((2 * RADIUS + 1) ** 2))

    def window_mean(k, r, step):
        lane = lanes_of(step)
        summed = add(*(get(p3, r + d, step, k) for d in (-3, 0, 3)))
        summed = add(summed, shifted(summed, 1, lane), shifted(summed, -1, lane))
        summed = add(summed, shifted(summed, 3, lane), shifted(summed, -3, lane))
        value = [x * scale for x in summed]
        put(tt, value, r, step, k)
        return value

    def three_first(r, step):
        for k in range(3):
            three_rows(k)(r, step)

    blocks(first, last, 16, three_first)

    def mean_first(r, step):
        for k in range(3):
            window_mean(k, r, step)

    blocks(16, total - 16, 16, mean_first)

    when_got(has_next, tile_b + forward_rows + forward_cols)
    unpack(b, next_left, next_right, 0)

    def change_block(r, step):
        change = [x - y for x, y in zip(get(b, r, step), get(a, r, step))]
        put(pr, [x * y for x, y in zip(get(gx, r, step), change)], r, step, 3)
        put(pr, [x * y for x, y in zip(get(gy, r, step), change)], r, step, 4)

    blocks(first, last, 32, change_block)

    def three_second(r, step):
        for k in (3, 4):
            three_rows(k)(r, step)

    blocks(first, last, 16, three_second)

    def tensor_block(r, step):
        lane = lanes_of(step)
        parts = [get(tt, r, step, k) for k in range(3)]
        parts += [window_mean(k, r, step) for k in (3, 4)]
        mid = get(q, r, step)
        around = add(
            get(q, r - 1, step), get(q, r + 1, step), shifted(mid, 1, lane), shifted(mid, -1, lane)
        )
        for k in range(nb):
            xx, xy, yy, xt, yt = (part[k] for part in parts)
            diag = mid[k] * around[k] + 2.0 * COUPLING
            one, two = xx + diag, yy + diag
            inverse = 1.0 / (one * two - xy * xy)
            ca, cb, cc = two * inverse, xy * inverse, one * inverse
            x, y = cb * yt - ca * xt, cb * xt - cc * yt
            at = pl.ds(r, step)
            for ref, value in ((va, ca), (vb, cb), (vc, cc)):
                ref[k, at, :] = value * COUPLING
            for ref, value in ((ua, ca), (ub, cb), (uc, cc)):
                ref[k, at, :] = value * mid[k]
            ex[k, at, :] = x
            ey[k, at, :] = y
            g0[0, k, at, :] = x * mid[k]
            g0[1, k, at, :] = y * mid[k]

    def relaxed(source, r, step, x, y):
        lane = lanes_of(step)

        def near(part):
            mid = get(source, r, step, part)
            return add(
                get(source, r - 1, step, part), get(source, r + 1, step, part),
                shifted(mid, 1, lane), shifted(mid, -1, lane),
            )

        nx, ny = near(0), near(1)
        ca, cb, cc = (get(ref, r, step) for ref in (ua, ub, uc))
        return (
            [x[k] + ca[k] * nx[k] - cb[k] * ny[k] for k in range(nb)],
            [y[k] + cc[k] * ny[k] - cb[k] * nx[k] for k in range(nb)],
        )

    def sweep(source, target, scaled=None):
        def body(r, step):
            new = relaxed(source, r, step, get(ex, r, step), get(ey, r, step))
            mid = get(q, r, step) if scaled is not None else None
            for part in range(2):
                if target is not None:
                    put(target, new[part], r, step, part)
                if scaled is not None:
                    put(scaled, [m * x for m, x in zip(mid, new[part])], r, step, part)

        return body

    bounds = list(range(first, last - CHUNK + 1, CHUNK)) + [last]
    chunks = len(bounds) - 1

    def stages(c, bodies, lead, ends):
        for k, body in enumerate(bodies):
            ahead = 8 * (lead - k)
            margin = ends[k == len(bodies) - 1]
            low = first + margin if c == 0 else bounds[c] + ahead
            high = last - margin if c == chunks - 1 else bounds[c + 1] + ahead
            blocks(low, high, 24, body)

    first_round = [tensor_block]
    now, other = g0, g1
    for k in range(1, SWEEPS):
        first_round.append(sweep(now, field if k == SWEEPS - 1 else None, other))
        now, other = other, now

    to_next, to_prev = [], []
    for c in range(chunks):
        stages(c, first_round, SWEEPS - 1, (8, 8))
        low, high = bounds[c], bounds[c + 1]
        folded = pl.ds((low - first) // FOLD, (high - low) // FOLD)
        pack_rim(field, rim, low, high, first, nw)
        rows_sent = pl.ds(max(low, 16), min(high, total - 16) - max(low, 16))

        def moves(rims, mains, device, way):
            pairs = (
                (rim.at[folded], rims.at[folded]),
                (field.at[:, main, rows_sent], mains.at[:, main, rows_sent]),
            )
            return [
                pltpu.make_async_remote_copy(
                    src_ref=src, dst_ref=dst, send_sem=chunk_send.at[way + i, c],
                    recv_sem=chunk_recv.at[way + i, c], device_id=device, device_id_type=MESH,
                )
                for i, (src, dst) in enumerate(pairs)
            ]

        to_next.append(moves(rim_before, main_before, next_id, 0))
        to_prev.append(moves(rim_after, main_after, prev_id, 2))
        when_start(has_next, to_next[c])
        when_start(has_prev, to_prev[c])

    put_tensor = [
        pltpu.make_async_copy(
            tt.at[:, k, inner], tensor_out.at[:, 0, :, columns(k)], local_sem.at[0, k]
        )
        for k in range(nw)
    ]
    for copy in put_tensor:
        copy.start()


    def first_block(r, step):
        at = pl.ds(r, step)

        def beside(part, ref):
            return [
                main_before[part, k, at, :] + main_after[part, k, at, :] for k in range(nw)
            ] + [ref[nw, at, :]]

        x, y = beside(0, gx), beside(1, gy)
        ca, cb, cc = (get(ref, r, step) for ref in (va, vb, vc))
        old_x, old_y = get(ex, r, step), get(ey, r, step)
        new_x = [old_x[k] + ca[k] * x[k] - cb[k] * y[k] for k in range(nb)]
        new_y = [old_y[k] + cc[k] * y[k] - cb[k] * x[k] for k in range(nb)]
        put(ex, new_x, r, step)
        put(ey, new_y, r, step)
        mid = get(q, r, step)
        for part, values in enumerate(relaxed(now, r, step, new_x, new_y)):
            put(other, [m * v for m, v in zip(mid, values)], r, step, part)

    second_round = [first_block]
    source, target = other, now
    for k in range(1, SWEEPS):
        if k == SWEEPS - 1:
            second_round.append(sweep(source, last_field))
        else:
            second_round.append(sweep(source, None, target))
        source, target = target, source

    for c in range(chunks):
        when_got(has_prev, to_next[c])
        when_got(has_next, to_prev[c])
        low, high = bounds[c], bounds[c + 1]
        size = (high - low) // FOLD
        folded = pl.ds((low - first) // FOLD, size)
        both = rim_before[folded, :] + rim_after[folded, :]
        lane = lanes_of(size)
        for j in range(FOLD):
            for k, ref in enumerate((gx, gy)):
                slot = (2 * j + k) * SLOT
                head = jnp.where(lane < 8, lane_roll(both, -slot), 0.0)
                tail = lane_roll(both, LANES - 16 - slot)
                ref[nw, pl.ds(low + j * size, size), :] = jnp.where(
                    lane >= LANES - 8, tail, head
                )
        stages(c, second_round, 0, (8, 16))

    for c in range(chunks):
        when_sent(has_next, to_next[c])
        when_sent(has_prev, to_prev[c])

    put_field = [
        pltpu.make_async_copy(
            last_field.at[:, k, inner], field_out.at[:, 0, :, columns(k)], local_sem.at[1, k]
        )
        for k in range(nw)
    ]
    for copy in put_field:
        copy.start()
    when_sent(has_up, up)
    when_sent(has_down, down)
    when_sent(has_right, [col_right])
    when_sent(has_left, [col_left])
    when_sent(has_prev, tile_b + forward_rows + forward_cols)
    for copy in put_tensor + put_field:
        copy.wait()


def pack_rim(field, rim, low, high, first, nw):
    size = (high - low) // FOLD
    lane = lax.broadcasted_iota(jnp.int32, (size, LANES), 1)
    out = jnp.zeros((size, LANES), jnp.float32)
    for j in range(FOLD):
        at = pl.ds(low + j * size, size)
        for k in range(2):
            slot = (2 * j + k) * SLOT
            block = field[k, nw, at, :]
            head, tail = lane_roll(block, slot), lane_roll(block, slot + SLOT)
            out = jnp.where((lane >= slot) & (lane < slot + 8), head, out)
            out = jnp.where((lane >= slot + 8) & (lane < slot + 16), tail, out)
    rim[pl.ds((low - first) // FOLD, size), :] = out


def local(counts, images, stiffness):
    _, rows, width = images.shape
    nw = width // LANES
    nb = nw + 1
    total = rows + 2 * EDGE
    f32 = jnp.float32
    plane = pltpu.VMEM((nb, total, LANES), f32)
    five = pltpu.VMEM((5, nb, total, LANES), f32)
    pair = pltpu.VMEM((2, nb, total, LANES), f32)
    packet = pltpu.VMEM(((total - 16) // FOLD, LANES), f32)
    mains = pltpu.VMEM((2, nw, total, LANES), f32)
    chunks = (total - 16) // CHUNK
    return pl.pallas_call(
        functools.partial(kernel, counts),
        out_shape=(
            jax.ShapeDtypeStruct((5, 1, rows, width), f32),
            jax.ShapeDtypeStruct((2, 1, rows, width), f32),
        ),
        in_specs=[pl.BlockSpec(memory_space=pltpu.HBM)] * 2,
        out_specs=[pl.BlockSpec(memory_space=pl.ANY)] * 2,
        scratch_shapes=[plane] * 6
        + [five] * 3
        + [plane] * 8
        + [pair] * 4
        + [packet] * 9
        + [mains] * 2
        + [
            pltpu.SemaphoreType.DMA((2, nw)),
            pltpu.SemaphoreType.DMA((KINDS, nw)),
            pltpu.SemaphoreType.DMA((KINDS, nw)),
            pltpu.SemaphoreType.DMA((4, chunks)),
            pltpu.SemaphoreType.DMA((4, chunks)),
        ],
        compiler_params=pltpu.CompilerParams(
            collective_id=0, has_side_effects=True, vmem_limit_bytes=67043328
        ),
    )(images, stiffness)


def solution(mesh):
    counts = tuple(mesh.shape[name] for name in ("sec", "row", "col"))
    spec = P("sec", "row", "col")
    out = P(None, "sec", "row", "col")
    return jax.shard_map(
        functools.partial(local, counts), mesh=mesh, in_specs=(spec, spec),
        out_specs=(out, out), check_vma=False,
    )
```

```python
import functools

import jax
import jax.numpy as jnp
from jax import lax
from jax.experimental import pallas as pl
from jax.experimental.pallas import tpu as pltpu
from jax.sharding import PartitionSpec as P

RADIUS = 4
SWEEPS = 4
ROUNDS = 2
COUPLING = 0.25
MESH = pl.DeviceIdType.MESH

LANES = 128
HALO = 16
EDGE = HALO + 8
SLOT = 16
CHUNK = 96
FOLD = LANES // (2 * SLOT)

(
    TILE_B, ROW_A_UP, ROW_A_DOWN, ROW_S_UP, ROW_S_DOWN, FWD_TOP, FWD_BOTTOM, COL_RIGHT, COL_LEFT,
    FWD_RIGHT, FWD_LEFT,
) = range(11)
KINDS = 11


def lane_roll(x, shift):
    return pltpu.roll(x, shift % x.shape[1], 1)


def shifted(blocks, shift, lane):
    rolled = [lane_roll(x, shift) for x in blocks]
    out = []
    for k, here in enumerate(rolled):
        if shift > 0:
            out.append(jnp.where(lane < shift, rolled[k - 1], here))
        else:
            out.append(jnp.where(lane >= LANES + shift, rolled[(k + 1) % len(rolled)], here))
    return out


def add(*terms):
    return [sum(xs[1:], xs[0]) for xs in zip(*terms)]


def kernel(
    counts, images, stiff, tensor_out, field_out,
    a, b, s, q, gx, gy, pr, p3, tt, ua, ub, uc, va, vb, vc, ex, ey, g0, g1, field, last_field,
    send_right, send_left, got_left, got_right, next_left, next_right,
    rim, rim_before, rim_after, main_before, main_after,
    local_sem, send_sem, recv_sem, chunk_send, chunk_recv,
):
    sec, row, col = (lax.axis_index(name) for name in ("sec", "row", "col"))
    n_sec, n_row, n_col = counts
    rows, width = images.shape[1], images.shape[2]
    nb, total, _ = a.shape
    nw = nb - 1
    has_prev, has_next = sec > 0, sec < n_sec - 1
    has_up, has_down = row > 0, row < n_row - 1
    has_left, has_right = col > 0, col < n_col - 1
    sides = (
        (has_prev, (sec - 1, row, col)), (has_next, (sec + 1, row, col)),
        (has_up, (sec, row - 1, col)), (has_down, (sec, row + 1, col)),
        (has_left, (sec, row, col - 1)), (has_right, (sec, row, col + 1)),
    )
    prev_id, next_id, up_id, down_id, left_id, right_id = (side[1] for side in sides)
    end = EDGE + rows
    first, last = 8, total - 8
    inner = pl.ds(EDGE, rows)
    main = pl.ds(0, nw)
    top, bottom = pl.ds(EDGE - HALO, HALO), pl.ds(end, HALO)
    piece = (last - first) // FOLD

    def remote(src, dst, k, device, part=0):
        return pltpu.make_async_remote_copy(
            src_ref=src, dst_ref=dst, send_sem=send_sem.at[k, part],
            recv_sem=recv_sem.at[k, part], device_id=device, device_id_type=MESH,
        )

    def columns(k):
        return pl.ds(k * LANES, LANES)

    loads = [
        pltpu.make_async_copy(src.at[0, :, columns(k)], dst.at[k, inner], local_sem.at[i, k])
        for i, (src, dst) in enumerate(((images, a), (stiff, s)))
        for k in range(nw)
    ]
    for copy in loads:
        copy.start()
    barrier = pltpu.get_barrier_semaphore()
    for there, device in sides:
        @pl.when(there)
        def _():
            pl.semaphore_signal(barrier, inc=1, device_id=device, device_id_type=MESH)

    def clear(ref):
        ref[...] = jnp.zeros(ref.shape, jnp.float32)

    @pl.when(jnp.logical_not(has_up))
    def _():
        clear(a.at[main, top])
        clear(s.at[main, top])

    @pl.when(jnp.logical_not(has_down))
    def _():
        clear(a.at[main, bottom])
        clear(s.at[main, bottom])

    @pl.when(jnp.logical_not(has_left))
    def _():
        clear(got_left)

    @pl.when(jnp.logical_not(has_right))
    def _():
        clear(got_right)

    @pl.when(jnp.logical_not(has_next))
    def _():
        clear(b)
        clear(next_left)
        clear(next_right)
        clear(rim_after)
        clear(main_after)

    @pl.when(jnp.logical_not(has_prev))
    def _():
        clear(rim_before)
        clear(main_before)

    for start in (0, total - 8):
        for ref in (a, q):
            clear(ref.at[:, pl.ds(start, 8)])
        for ref in (pr, p3):
            clear(ref.at[:, :, pl.ds(start, 8)])
    for start in (8, total - 16):
        for ref in (g0, g1, field):
            clear(ref.at[:, :, pl.ds(start, 8)])

    pl.semaphore_wait(barrier, sum(jnp.where(there, 1, 0) for there, _device in sides))

    def by_block(src, at, dst, to, k, device):
        return [
            remote(src.at[0, at, columns(p)], dst.at[p, to], k, device, p) for p in range(nw)
        ]

    low, high = pl.ds(0, HALO), pl.ds(rows - HALO, HALO)
    tile_b = by_block(images, pl.ds(0, rows), b, inner, TILE_B, prev_id)
    up = by_block(stiff, low, s, bottom, ROW_S_UP, up_id)
    up += by_block(images, low, a, bottom, ROW_A_UP, up_id)
    down = by_block(stiff, high, s, top, ROW_S_DOWN, down_id)
    down += by_block(images, high, a, top, ROW_A_DOWN, down_id)
    col_right = remote(send_right, got_left, COL_RIGHT, right_id)
    col_left = remote(send_left, got_right, COL_LEFT, left_id)
    forward_rows = [
        remote(a.at[main, top], b.at[main, top], FWD_TOP, prev_id),
        remote(a.at[main, bottom], b.at[main, bottom], FWD_BOTTOM, prev_id),
    ]
    forward_cols = [
        remote(got_left, next_left, FWD_LEFT, prev_id),
        remote(got_right, next_right, FWD_RIGHT, prev_id),
    ]

    def when_start(there, copies):
        @pl.when(there)
        def _():
            for copy in copies:
                copy.start()

    def when_got(there, copies):
        @pl.when(there)
        def _():
            for copy in copies:
                copy.wait_recv()

    def when_sent(there, copies):
        @pl.when(there)
        def _():
            for copy in copies:
                copy.wait_send()

    when_start(has_up, up)
    when_start(has_down, down)
    when_start(has_prev, tile_b)
    for copy in loads:
        copy.wait()
    when_got(has_up, down)
    when_got(has_down, up)
    when_start(has_prev, forward_rows)

    def lanes_of(count):
        return lax.broadcasted_iota(jnp.int32, (count, LANES), 1)

    lane = lanes_of(piece)

    def packed(block, at):
        out = jnp.zeros((piece, LANES), jnp.float32)
        for j in range(FOLD):
            span = pl.ds(first + j * piece, piece)
            for k, ref in enumerate((a, s)):
                low = (2 * j + k) * SLOT
                moved = lane_roll(ref[block, span, :], low - at)
                out = jnp.where((lane >= low) & (lane < low + SLOT), moved, out)
        return out

    def unpack(ref, left, right, k):
        for j in range(FOLD):
            low = (2 * j + k) * SLOT
            from_right = jnp.where(lane < SLOT, lane_roll(right[...], -low), 0.0)
            from_left = lane_roll(left[...], LANES - SLOT - low)
            ref[nw, pl.ds(first + j * piece, piece), :] = jnp.where(
                lane >= LANES - SLOT, from_left, from_right
            )

    @pl.when(has_right)
    def _():
        send_right[...] = packed(nw - 1, LANES - SLOT)
        col_right.start()

    @pl.when(has_left)
    def _():
        send_left[...] = packed(0, 0)
        col_left.start()

    when_got(has_left, [col_right])
    when_got(has_right, [col_left])
    when_start(has_prev, forward_cols)
    unpack(a, got_left, got_right, 0)
    unpack(s, got_left, got_right, 1)

    def blocks(low, high, step, body):
        def one(i, carry):
            body(pl.multiple_of(low + i * step, 8), step)
            return carry

        count = (high - low) // step
        lax.fori_loop(0, count, one, 0)
        rest = high - low - count * step
        if rest:
            body(low + count * step, rest)

    def get(ref, r, step, *lead):
        return [ref[(*lead, k, pl.ds(r, step), slice(None))] for k in range(nb)]

    def put(ref, values, r, step, *lead):
        for k, value in enumerate(values):
            ref[(*lead, k, pl.ds(r, step), slice(None))] = value

    def gradient_block(r, step):
        lane = lanes_of(step)
        rr = lax.broadcasted_iota(jnp.int32, (step, LANES), 0) + r
        row_ok = ((rr >= EDGE) | has_up) & ((rr < end) | has_down)
        rim_ok = ((lane < LANES // 2) & has_right) | ((lane >= LANES // 2) & has_left)
        masks = [row_ok] * nw + [row_ok & rim_ok]
        mid = get(a, r, step)
        after, before = shifted(mid, -1, lane), shifted(mid, 1, lane)
        under, over = get(a, r + 1, step), get(a, r - 1, step)
        dx = [jnp.where(m, (x - y) * 0.5, 0.0) for m, x, y in zip(masks, after, before)]
        dy = [jnp.where(m, (x - y) * 0.5, 0.0) for m, x, y in zip(masks, under, over)]
        put(gx, dx, r, step)
        put(gy, dy, r, step)
        put(pr, [x * x for x in dx], r, step, 0)
        put(pr, [x * y for x, y in zip(dx, dy)], r, step, 1)
        put(pr, [y * y for y in dy], r, step, 2)
        put(q, [jnp.sqrt(x) for x in get(s, r, step)], r, step)

    blocks(first, last, 16, gradient_block)

    def three_rows(k):
        def body(r, step):
            put(p3, add(*(get(pr, r + d, step, k) for d in (-1, 0, 1))), r, step, k)

        return body

    scale = jnp.where(has_next, jnp.float32(1.0), jnp.float32(0.0))
    scale = scale * (1.0 / float((2 * RADIUS + 1) ** 2))

    def window_mean(k, r, step):
        lane = lanes_of(step)
        summed = add(*(get(p3, r + d, step, k) for d in (-3, 0, 3)))
        summed = add(summed, shifted(summed, 1, lane), shifted(summed, -1, lane))
        summed = add(summed, shifted(summed, 3, lane), shifted(summed, -3, lane))
        value = [x * scale for x in summed]
        put(tt, value, r, step, k)
        return value

    def three_first(r, step):
        for k in range(3):
            three_rows(k)(r, step)

    blocks(first, last, 16, three_first)

    def mean_first(r, step):
        for k in range(3):
            window_mean(k, r, step)

    blocks(16, total - 16, 16, mean_first)

    when_got(has_next, tile_b + forward_rows + forward_cols)
    unpack(b, next_left, next_right, 0)

    def change_block(r, step):
        change = [x - y for x, y in zip(get(b, r, step), get(a, r, step))]
        put(pr, [x * y for x, y in zip(get(gx, r, step), change)], r, step, 3)
        put(pr, [x * y for x, y in zip(get(gy, r, step), change)], r, step, 4)

    blocks(first, last, 32, change_block)

    def three_second(r, step):
        for k in (3, 4):
            three_rows(k)(r, step)

    blocks(first, last, 16, three_second)

    def tensor_block(r, step):
        lane = lanes_of(step)
        parts = [get(tt, r, step, k) for k in range(3)]
        parts += [window_mean(k, r, step) for k in (3, 4)]
        mid = get(q, r, step)
        around = add(
            get(q, r - 1, step), get(q, r + 1, step), shifted(mid, 1, lane), shifted(mid, -1, lane)
        )
        for k in range(nb):
            xx, xy, yy, xt, yt = (part[k] for part in parts)
            diag = mid[k] * around[k] + 2.0 * COUPLING
            one, two = xx + diag, yy + diag
            inverse = 1.0 / (one * two - xy * xy)
            ca, cb, cc = two * inverse, xy * inverse, one * inverse
            x, y = cb * yt - ca * xt, cb * xt - cc * yt
            at = pl.ds(r, step)
            for ref, value in ((va, ca), (vb, cb), (vc, cc)):
                ref[k, at, :] = value * COUPLING
            for ref, value in ((ua, ca), (ub, cb), (uc, cc)):
                ref[k, at, :] = value * mid[k]
            ex[k, at, :] = x
            ey[k, at, :] = y
            g0[0, k, at, :] = x * mid[k]
            g0[1, k, at, :] = y * mid[k]

    def relaxed(source, r, step, x, y):
        lane = lanes_of(step)

        def near(part):
            mid = get(source, r, step, part)
            return add(
                get(source, r - 1, step, part), get(source, r + 1, step, part),
                shifted(mid, 1, lane), shifted(mid, -1, lane),
            )

        nx, ny = near(0), near(1)
        ca, cb, cc = (get(ref, r, step) for ref in (ua, ub, uc))
        return (
            [x[k] + ca[k] * nx[k] - cb[k] * ny[k] for k in range(nb)],
            [y[k] + cc[k] * ny[k] - cb[k] * nx[k] for k in range(nb)],
        )

    def sweep(source, target, scaled=None):
        def body(r, step):
            new = relaxed(source, r, step, get(ex, r, step), get(ey, r, step))
            mid = get(q, r, step) if scaled is not None else None
            for part in range(2):
                if target is not None:
                    put(target, new[part], r, step, part)
                if scaled is not None:
                    put(scaled, [m * x for m, x in zip(mid, new[part])], r, step, part)

        return body

    bounds = list(range(first, last - CHUNK + 1, CHUNK)) + [last]
    chunks = len(bounds) - 1

    def stages(c, bodies, lead, ends):
        for k, body in enumerate(bodies):
            ahead = 8 * (lead - k)
            margin = ends[k == len(bodies) - 1]
            low = first + margin if c == 0 else bounds[c] + ahead
            high = last - margin if c == chunks - 1 else bounds[c + 1] + ahead
            blocks(low, high, 24, body)

    first_round = [tensor_block]
    now, other = g0, g1
    for k in range(1, SWEEPS):
        first_round.append(sweep(now, field if k == SWEEPS - 1 else None, other))
        now, other = other, now

    to_next, to_prev = [], []
    for c in range(chunks):
        stages(c, first_round, SWEEPS - 1, (8, 8))
        low, high = bounds[c], bounds[c + 1]
        folded = pl.ds((low - first) // FOLD, (high - low) // FOLD)
        pack_rim(field, rim, low, high, first, nw)
        rows_sent = pl.ds(max(low, 16), min(high, total - 16) - max(low, 16))

        def moves(rims, mains, device, way):
            pairs = (
                (rim.at[folded], rims.at[folded]),
                (field.at[:, main, rows_sent], mains.at[:, main, rows_sent]),
            )
            return [
                pltpu.make_async_remote_copy(
                    src_ref=src, dst_ref=dst, send_sem=chunk_send.at[way + i, c],
                    recv_sem=chunk_recv.at[way + i, c], device_id=device, device_id_type=MESH,
                )
                for i, (src, dst) in enumerate(pairs)
            ]

        to_next.append(moves(rim_before, main_before, next_id, 0))
        to_prev.append(moves(rim_after, main_after, prev_id, 2))
        when_start(has_next, to_next[c])
        when_start(has_prev, to_prev[c])

    put_tensor = [
        pltpu.make_async_copy(
            tt.at[:, k, inner], tensor_out.at[:, 0, :, columns(k)], local_sem.at[0, k]
        )
        for k in range(nw)
    ]
    for copy in put_tensor:
        copy.start()


    def first_block(r, step):
        at = pl.ds(r, step)

        def beside(part, ref):
            return [
                main_before[part, k, at, :] + main_after[part, k, at, :] for k in range(nw)
            ] + [ref[nw, at, :]]

        x, y = beside(0, gx), beside(1, gy)
        ca, cb, cc = (get(ref, r, step) for ref in (va, vb, vc))
        old_x, old_y = get(ex, r, step), get(ey, r, step)
        new_x = [old_x[k] + ca[k] * x[k] - cb[k] * y[k] for k in range(nb)]
        new_y = [old_y[k] + cc[k] * y[k] - cb[k] * x[k] for k in range(nb)]
        put(ex, new_x, r, step)
        put(ey, new_y, r, step)
        mid = get(q, r, step)
        for part, values in enumerate(relaxed(now, r, step, new_x, new_y)):
            put(other, [m * v for m, v in zip(mid, values)], r, step, part)

    second_round = [first_block]
    source, target = other, now
    for k in range(1, SWEEPS):
        if k == SWEEPS - 1:
            second_round.append(sweep(source, last_field))
        else:
            second_round.append(sweep(source, None, target))
        source, target = target, source

    for c in range(chunks):
        when_got(has_prev, to_next[c])
        when_got(has_next, to_prev[c])
        low, high = bounds[c], bounds[c + 1]
        size = (high - low) // FOLD
        folded = pl.ds((low - first) // FOLD, size)
        both = rim_before[folded, :] + rim_after[folded, :]
        lane = lanes_of(size)
        for j in range(FOLD):
            for k, ref in enumerate((gx, gy)):
                slot = (2 * j + k) * SLOT
                head = jnp.where(lane < 8, lane_roll(both, -slot), 0.0)
                tail = lane_roll(both, LANES - 16 - slot)
                ref[nw, pl.ds(low + j * size, size), :] = jnp.where(
                    lane >= LANES - 8, tail, head
                )
        stages(c, second_round, 0, (8, 16))

    for c in range(chunks):
        when_sent(has_next, to_next[c])
        when_sent(has_prev, to_prev[c])

    put_field = [
        pltpu.make_async_copy(
            last_field.at[:, k, inner], field_out.at[:, 0, :, columns(k)], local_sem.at[1, k]
        )
        for k in range(nw)
    ]
    for copy in put_field:
        copy.start()
    when_sent(has_up, up)
    when_sent(has_down, down)
    when_sent(has_right, [col_right])
    when_sent(has_left, [col_left])
    when_sent(has_prev, tile_b + forward_rows + forward_cols)
    for copy in put_tensor + put_field:
        copy.wait()


def pack_rim(field, rim, low, high, first, nw):
    size = (high - low) // FOLD
    lane = lax.broadcasted_iota(jnp.int32, (size, LANES), 1)
    out = jnp.zeros((size, LANES), jnp.float32)
    for j in range(FOLD):
        at = pl.ds(low + j * size, size)
        for k in range(2):
            slot = (2 * j + k) * SLOT
            block = field[k, nw, at, :]
            head, tail = lane_roll(block, slot), lane_roll(block, slot + SLOT)
            out = jnp.where((lane >= slot) & (lane < slot + 8), head, out)
            out = jnp.where((lane >= slot + 8) & (lane < slot + 16), tail, out)
    rim[pl.ds((low - first) // FOLD, size), :] = out


def local(counts, images, stiffness):
    _, rows, width = images.shape
    nw = width // LANES
    nb = nw + 1
    total = rows + 2 * EDGE
    f32 = jnp.float32
    plane = pltpu.VMEM((nb, total, LANES), f32)
    five = pltpu.VMEM((5, nb, total, LANES), f32)
    pair = pltpu.VMEM((2, nb, total, LANES), f32)
    packet = pltpu.VMEM(((total - 16) // FOLD, LANES), f32)
    mains = pltpu.VMEM((2, nw, total, LANES), f32)
    chunks = (total - 16) // CHUNK
    return pl.pallas_call(
        functools.partial(kernel, counts),
        out_shape=(
            jax.ShapeDtypeStruct((5, 1, rows, width), f32),
            jax.ShapeDtypeStruct((2, 1, rows, width), f32),
        ),
        in_specs=[pl.BlockSpec(memory_space=pltpu.HBM)] * 2,
        out_specs=[pl.BlockSpec(memory_space=pl.ANY)] * 2,
        scratch_shapes=[plane] * 6
        + [five] * 3
        + [plane] * 8
        + [pair] * 4
        + [packet] * 9
        + [mains] * 2
        + [
            pltpu.SemaphoreType.DMA((2, nw)),
            pltpu.SemaphoreType.DMA((KINDS, nw)),
            pltpu.SemaphoreType.DMA((KINDS, nw)),
            pltpu.SemaphoreType.DMA((4, chunks)),
            pltpu.SemaphoreType.DMA((4, chunks)),
        ],
        compiler_params=pltpu.CompilerParams(
            collective_id=0, has_side_effects=True, vmem_limit_bytes=48 * 1024 * 1024
        ),
    )(*(pltpu.with_memory_space_constraint(x, pltpu.HBM) for x in (images, stiffness)))


def solution(mesh):
    counts = tuple(mesh.shape[name] for name in ("sec", "row", "col"))
    spec = P("sec", "row", "col")
    out = P(None, "sec", "row", "col")
    return jax.shard_map(
        functools.partial(local, counts), mesh=mesh, in_specs=(spec, spec),
        out_specs=(out, out), check_vma=False,
    )
```

```python
import functools

import jax
import jax.numpy as jnp
from jax import lax
from jax.experimental import pallas as pl
from jax.experimental.pallas import tpu as pltpu
from jax.sharding import PartitionSpec as P

RADIUS = 4
SWEEPS = 4
ROUNDS = 2
COUPLING = 0.25
MESH = pl.DeviceIdType.MESH

LANES = 128
HALO = 16
EDGE = HALO + 8
SLOT = 16
CHUNK = 64
FOLD = LANES // (2 * SLOT)

(
    TILE_B, ROW_A_UP, ROW_A_DOWN, ROW_S_UP, ROW_S_DOWN, FWD_TOP, FWD_BOTTOM, COL_RIGHT, COL_LEFT,
    FWD_RIGHT, FWD_LEFT,
) = range(11)
KINDS = 11


def lane_roll(x, shift):
    return pltpu.roll(x, shift % x.shape[1], 1)


def shifted(blocks, shift, lane):
    rolled = [lane_roll(x, shift) for x in blocks]
    out = []
    for k, here in enumerate(rolled):
        if shift > 0:
            out.append(jnp.where(lane < shift, rolled[k - 1], here))
        else:
            out.append(jnp.where(lane >= LANES + shift, rolled[(k + 1) % len(rolled)], here))
    return out


def add(*terms):
    return [sum(xs[1:], xs[0]) for xs in zip(*terms)]


def kernel(
    counts, images, stiff, tensor_out, field_out,
    a, b, s, q, gx, gy, pr, p3, tt, ua, ub, uc, va, vb, vc, ex, ey, g0, g1, field, last_field,
    send_right, send_left, got_left, got_right, next_left, next_right,
    rim, rim_before, rim_after, main_before, main_after,
    local_sem, send_sem, recv_sem, chunk_send, chunk_recv,
):
    sec, row, col = (lax.axis_index(name) for name in ("sec", "row", "col"))
    n_sec, n_row, n_col = counts
    rows, width = images.shape[1], images.shape[2]
    nb, total, _ = a.shape
    nw = nb - 1
    has_prev, has_next = sec > 0, sec < n_sec - 1
    has_up, has_down = row > 0, row < n_row - 1
    has_left, has_right = col > 0, col < n_col - 1
    sides = (
        (has_prev, (sec - 1, row, col)), (has_next, (sec + 1, row, col)),
        (has_up, (sec, row - 1, col)), (has_down, (sec, row + 1, col)),
        (has_left, (sec, row, col - 1)), (has_right, (sec, row, col + 1)),
    )
    prev_id, next_id, up_id, down_id, left_id, right_id = (side[1] for side in sides)
    end = EDGE + rows
    first, last = 8, total - 8
    inner = pl.ds(EDGE, rows)
    main = pl.ds(0, nw)
    top, bottom = pl.ds(EDGE - HALO, HALO), pl.ds(end, HALO)
    piece = (last - first) // FOLD

    def remote(src, dst, k, device, part=0):
        return pltpu.make_async_remote_copy(
            src_ref=src, dst_ref=dst, send_sem=send_sem.at[k, part],
            recv_sem=recv_sem.at[k, part], device_id=device, device_id_type=MESH,
        )

    def columns(k):
        return pl.ds(k * LANES, LANES)

    loads = [
        pltpu.make_async_copy(src.at[0, :, columns(k)], dst.at[k, inner], local_sem.at[i, k])
        for i, (src, dst) in enumerate(((images, a), (stiff, s)))
        for k in range(nw)
    ]
    for copy in loads:
        copy.start()
    barrier = pltpu.get_barrier_semaphore()
    for there, device in sides:
        @pl.when(there)
        def _():
            pl.semaphore_signal(barrier, inc=1, device_id=device, device_id_type=MESH)

    def clear(ref):
        ref[...] = jnp.zeros(ref.shape, jnp.float32)

    @pl.when(jnp.logical_not(has_up))
    def _():
        clear(a.at[main, top])
        clear(s.at[main, top])

    @pl.when(jnp.logical_not(has_down))
    def _():
        clear(a.at[main, bottom])
        clear(s.at[main, bottom])

    @pl.when(jnp.logical_not(has_left))
    def _():
        clear(got_left)

    @pl.when(jnp.logical_not(has_right))
    def _():
        clear(got_right)

    @pl.when(jnp.logical_not(has_next))
    def _():
        clear(b)
        clear(next_left)
        clear(next_right)
        clear(rim_after)
        clear(main_after)

    @pl.when(jnp.logical_not(has_prev))
    def _():
        clear(rim_before)
        clear(main_before)

    for start in (0, total - 8):
        for ref in (a, q):
            clear(ref.at[:, pl.ds(start, 8)])
        for ref in (pr, p3):
            clear(ref.at[:, :, pl.ds(start, 8)])
    for start in (8, total - 16):
        for ref in (g0, g1, field):
            clear(ref.at[:, :, pl.ds(start, 8)])

    pl.semaphore_wait(barrier, sum(jnp.where(there, 1, 0) for there, _device in sides))

    def by_block(src, at, dst, to, k, device):
        return [
            remote(src.at[0, at, columns(p)], dst.at[p, to], k, device, p) for p in range(nw)
        ]

    low, high = pl.ds(0, HALO), pl.ds(rows - HALO, HALO)
    tile_b = by_block(images, pl.ds(0, rows), b, inner, TILE_B, prev_id)
    up = by_block(stiff, low, s, bottom, ROW_S_UP, up_id)
    up += by_block(images, low, a, bottom, ROW_A_UP, up_id)
    down = by_block(stiff, high, s, top, ROW_S_DOWN, down_id)
    down += by_block(images, high, a, top, ROW_A_DOWN, down_id)
    col_right = remote(send_right, got_left, COL_RIGHT, right_id)
    col_left = remote(send_left, got_right, COL_LEFT, left_id)
    forward_rows = [
        remote(a.at[main, top], b.at[main, top], FWD_TOP, prev_id),
        remote(a.at[main, bottom], b.at[main, bottom], FWD_BOTTOM, prev_id),
    ]
    forward_cols = [
        remote(got_left, next_left, FWD_LEFT, prev_id),
        remote(got_right, next_right, FWD_RIGHT, prev_id),
    ]

    def when_start(there, copies):
        @pl.when(there)
        def _():
            for copy in copies:
                copy.start()

    def when_got(there, copies):
        @pl.when(there)
        def _():
            for copy in copies:
                copy.wait_recv()

    def when_sent(there, copies):
        @pl.when(there)
        def _():
            for copy in copies:
                copy.wait_send()

    when_start(has_up, up)
    when_start(has_down, down)
    when_start(has_prev, tile_b)
    for copy in loads:
        copy.wait()
    when_got(has_up, down)
    when_got(has_down, up)
    when_start(has_prev, forward_rows)

    def lanes_of(count):
        return lax.broadcasted_iota(jnp.int32, (count, LANES), 1)

    lane = lanes_of(piece)

    def packed(block, at):
        out = jnp.zeros((piece, LANES), jnp.float32)
        for j in range(FOLD):
            span = pl.ds(first + j * piece, piece)
            for k, ref in enumerate((a, s)):
                low = (2 * j + k) * SLOT
                moved = lane_roll(ref[block, span, :], low - at)
                out = jnp.where((lane >= low) & (lane < low + SLOT), moved, out)
        return out

    def unpack(ref, left, right, k):
        for j in range(FOLD):
            low = (2 * j + k) * SLOT
            from_right = jnp.where(lane < SLOT, lane_roll(right[...], -low), 0.0)
            from_left = lane_roll(left[...], LANES - SLOT - low)
            ref[nw, pl.ds(first + j * piece, piece), :] = jnp.where(
                lane >= LANES - SLOT, from_left, from_right
            )

    @pl.when(has_right)
    def _():
        send_right[...] = packed(nw - 1, LANES - SLOT)
        col_right.start()

    @pl.when(has_left)
    def _():
        send_left[...] = packed(0, 0)
        col_left.start()

    when_got(has_left, [col_right])
    when_got(has_right, [col_left])
    when_start(has_prev, forward_cols)
    unpack(a, got_left, got_right, 0)
    unpack(s, got_left, got_right, 1)

    def blocks(low, high, step, body):
        def one(i, carry):
            body(pl.multiple_of(low + i * step, 8), step)
            return carry

        count = (high - low) // step
        lax.fori_loop(0, count, one, 0)
        rest = high - low - count * step
        if rest:
            body(low + count * step, rest)

    def get(ref, r, step, *lead):
        return [ref[(*lead, k, pl.ds(r, step), slice(None))] for k in range(nb)]

    def put(ref, values, r, step, *lead):
        for k, value in enumerate(values):
            ref[(*lead, k, pl.ds(r, step), slice(None))] = value

    def gradient_block(r, step):
        lane = lanes_of(step)
        rr = lax.broadcasted_iota(jnp.int32, (step, LANES), 0) + r
        row_ok = ((rr >= EDGE) | has_up) & ((rr < end) | has_down)
        rim_ok = ((lane < LANES // 2) & has_right) | ((lane >= LANES // 2) & has_left)
        masks = [row_ok] * nw + [row_ok & rim_ok]
        mid = get(a, r, step)
        after, before = shifted(mid, -1, lane), shifted(mid, 1, lane)
        under, over = get(a, r + 1, step), get(a, r - 1, step)
        dx = [jnp.where(m, (x - y) * 0.5, 0.0) for m, x, y in zip(masks, after, before)]
        dy = [jnp.where(m, (x - y) * 0.5, 0.0) for m, x, y in zip(masks, under, over)]
        put(gx, dx, r, step)
        put(gy, dy, r, step)
        put(pr, [x * x for x in dx], r, step, 0)
        put(pr, [x * y for x, y in zip(dx, dy)], r, step, 1)
        put(pr, [y * y for y in dy], r, step, 2)
        put(q, [jnp.sqrt(x) for x in get(s, r, step)], r, step)

    blocks(first, last, 16, gradient_block)

    def three_rows(k):
        def body(r, step):
            put(p3, add(*(get(pr, r + d, step, k) for d in (-1, 0, 1))), r, step, k)

        return body

    scale = jnp.where(has_next, jnp.float32(1.0), jnp.float32(0.0))
    scale = scale * (1.0 / float((2 * RADIUS + 1) ** 2))

    def window_mean(k, r, step):
        lane = lanes_of(step)
        summed = add(*(get(p3, r + d, step, k) for d in (-3, 0, 3)))
        summed = add(summed, shifted(summed, 1, lane), shifted(summed, -1, lane))
        summed = add(summed, shifted(summed, 3, lane), shifted(summed, -3, lane))
        value = [x * scale for x in summed]
        put(tt, value, r, step, k)
        return value

    def three_first(r, step):
        for k in range(3):
            three_rows(k)(r, step)

    blocks(first, last, 16, three_first)

    def mean_first(r, step):
        for k in range(3):
            window_mean(k, r, step)

    blocks(16, total - 16, 16, mean_first)

    when_got(has_next, tile_b + forward_rows + forward_cols)
    unpack(b, next_left, next_right, 0)

    def change_block(r, step):
        change = [x - y for x, y in zip(get(b, r, step), get(a, r, step))]
        put(pr, [x * y for x, y in zip(get(gx, r, step), change)], r, step, 3)
        put(pr, [x * y for x, y in zip(get(gy, r, step), change)], r, step, 4)

    blocks(first, last, 32, change_block)

    def three_second(r, step):
        for k in (3, 4):
            three_rows(k)(r, step)

    blocks(first, last, 16, three_second)

    def tensor_block(r, step):
        lane = lanes_of(step)
        parts = [get(tt, r, step, k) for k in range(3)]
        parts += [window_mean(k, r, step) for k in (3, 4)]
        mid = get(q, r, step)
        around = add(
            get(q, r - 1, step), get(q, r + 1, step), shifted(mid, 1, lane), shifted(mid, -1, lane)
        )
        for k in range(nb):
            xx, xy, yy, xt, yt = (part[k] for part in parts)
            diag = mid[k] * around[k] + 2.0 * COUPLING
            one, two = xx + diag, yy + diag
            inverse = 1.0 / (one * two - xy * xy)
            ca, cb, cc = two * inverse, xy * inverse, one * inverse
            x, y = cb * yt - ca * xt, cb * xt - cc * yt
            at = pl.ds(r, step)
            for ref, value in ((va, ca), (vb, cb), (vc, cc)):
                ref[k, at, :] = value * COUPLING
            for ref, value in ((ua, ca), (ub, cb), (uc, cc)):
                ref[k, at, :] = value * mid[k]
            ex[k, at, :] = x
            ey[k, at, :] = y
            g0[0, k, at, :] = x * mid[k]
            g0[1, k, at, :] = y * mid[k]

    def relaxed(source, r, step, x, y):
        lane = lanes_of(step)

        def near(part):
            mid = get(source, r, step, part)
            return add(
                get(source, r - 1, step, part), get(source, r + 1, step, part),
                shifted(mid, 1, lane), shifted(mid, -1, lane),
            )

        nx, ny = near(0), near(1)
        ca, cb, cc = (get(ref, r, step) for ref in (ua, ub, uc))
        return (
            [x[k] + ca[k] * nx[k] - cb[k] * ny[k] for k in range(nb)],
            [y[k] + cc[k] * ny[k] - cb[k] * nx[k] for k in range(nb)],
        )

    def sweep(source, target, scaled=None):
        def body(r, step):
            new = relaxed(source, r, step, get(ex, r, step), get(ey, r, step))
            mid = get(q, r, step) if scaled is not None else None
            for part in range(2):
                if target is not None:
                    put(target, new[part], r, step, part)
                if scaled is not None:
                    put(scaled, [m * x for m, x in zip(mid, new[part])], r, step, part)

        return body

    bounds = list(range(first, last - CHUNK + 1, CHUNK)) + [last]
    chunks = len(bounds) - 1

    def stages(c, bodies, lead, ends):
        for k, body in enumerate(bodies):
            ahead = 8 * (lead - k)
            margin = ends[k == len(bodies) - 1]
            low = first + margin if c == 0 else bounds[c] + ahead
            high = last - margin if c == chunks - 1 else bounds[c + 1] + ahead
            blocks(low, high, 32, body)

    first_round = [tensor_block]
    now, other = g0, g1
    for k in range(1, SWEEPS):
        first_round.append(sweep(now, field if k == SWEEPS - 1 else None, other))
        now, other = other, now

    to_next, to_prev = [], []
    for c in range(chunks):
        stages(c, first_round, SWEEPS - 1, (8, 8))
        low, high = bounds[c], bounds[c + 1]
        folded = pl.ds((low - first) // FOLD, (high - low) // FOLD)
        pack_rim(field, rim, low, high, first, nw)
        rows_sent = pl.ds(max(low, 16), min(high, total - 16) - max(low, 16))

        def moves(rims, mains, device, way):
            pairs = (
                (rim.at[folded], rims.at[folded]),
                (field.at[:, main, rows_sent], mains.at[:, main, rows_sent]),
            )
            return [
                pltpu.make_async_remote_copy(
                    src_ref=src, dst_ref=dst, send_sem=chunk_send.at[way + i, c],
                    recv_sem=chunk_recv.at[way + i, c], device_id=device, device_id_type=MESH,
                )
                for i, (src, dst) in enumerate(pairs)
            ]

        to_next.append(moves(rim_before, main_before, next_id, 0))
        to_prev.append(moves(rim_after, main_after, prev_id, 2))
        when_start(has_next, to_next[c])
        when_start(has_prev, to_prev[c])

    put_tensor = [
        pltpu.make_async_copy(
            tt.at[:, k, inner], tensor_out.at[:, 0, :, columns(k)], local_sem.at[0, k]
        )
        for k in range(nw)
    ]
    for copy in put_tensor:
        copy.start()


    def first_block(r, step):
        at = pl.ds(r, step)

        def beside(part, ref):
            return [
                main_before[part, k, at, :] + main_after[part, k, at, :] for k in range(nw)
            ] + [ref[nw, at, :]]

        x, y = beside(0, gx), beside(1, gy)
        ca, cb, cc = (get(ref, r, step) for ref in (va, vb, vc))
        old_x, old_y = get(ex, r, step), get(ey, r, step)
        new_x = [old_x[k] + ca[k] * x[k] - cb[k] * y[k] for k in range(nb)]
        new_y = [old_y[k] + cc[k] * y[k] - cb[k] * x[k] for k in range(nb)]
        put(ex, new_x, r, step)
        put(ey, new_y, r, step)
        mid = get(q, r, step)
        for part, values in enumerate(relaxed(now, r, step, new_x, new_y)):
            put(other, [m * v for m, v in zip(mid, values)], r, step, part)

    second_round = [first_block]
    source, target = other, now
    for k in range(1, SWEEPS):
        if k == SWEEPS - 1:
            second_round.append(sweep(source, last_field))
        else:
            second_round.append(sweep(source, None, target))
        source, target = target, source

    for c in range(chunks):
        when_got(has_prev, to_next[c])
        when_got(has_next, to_prev[c])
        low, high = bounds[c], bounds[c + 1]
        size = (high - low) // FOLD
        folded = pl.ds((low - first) // FOLD, size)
        both = rim_before[folded, :] + rim_after[folded, :]
        lane = lanes_of(size)
        for j in range(FOLD):
            for k, ref in enumerate((gx, gy)):
                slot = (2 * j + k) * SLOT
                head = jnp.where(lane < 8, lane_roll(both, -slot), 0.0)
                tail = lane_roll(both, LANES - 16 - slot)
                ref[nw, pl.ds(low + j * size, size), :] = jnp.where(
                    lane >= LANES - 8, tail, head
                )
        stages(c, second_round, 0, (8, 16))

    for c in range(chunks):
        when_sent(has_next, to_next[c])
        when_sent(has_prev, to_prev[c])

    put_field = [
        pltpu.make_async_copy(
            last_field.at[:, k, inner], field_out.at[:, 0, :, columns(k)], local_sem.at[1, k]
        )
        for k in range(nw)
    ]
    for copy in put_field:
        copy.start()
    when_sent(has_up, up)
    when_sent(has_down, down)
    when_sent(has_right, [col_right])
    when_sent(has_left, [col_left])
    when_sent(has_prev, tile_b + forward_rows + forward_cols)
    for copy in put_tensor + put_field:
        copy.wait()


def pack_rim(field, rim, low, high, first, nw):
    size = (high - low) // FOLD
    lane = lax.broadcasted_iota(jnp.int32, (size, LANES), 1)
    out = jnp.zeros((size, LANES), jnp.float32)
    for j in range(FOLD):
        at = pl.ds(low + j * size, size)
        for k in range(2):
            slot = (2 * j + k) * SLOT
            block = field[k, nw, at, :]
            head, tail = lane_roll(block, slot), lane_roll(block, slot + SLOT)
            out = jnp.where((lane >= slot) & (lane < slot + 8), head, out)
            out = jnp.where((lane >= slot + 8) & (lane < slot + 16), tail, out)
    rim[pl.ds((low - first) // FOLD, size), :] = out


def local(counts, images, stiffness):
    _, rows, width = images.shape
    nw = width // LANES
    nb = nw + 1
    total = rows + 2 * EDGE
    f32 = jnp.float32
    plane = pltpu.VMEM((nb, total, LANES), f32)
    five = pltpu.VMEM((5, nb, total, LANES), f32)
    pair = pltpu.VMEM((2, nb, total, LANES), f32)
    packet = pltpu.VMEM(((total - 16) // FOLD, LANES), f32)
    mains = pltpu.VMEM((2, nw, total, LANES), f32)
    chunks = (total - 16) // CHUNK
    return pl.pallas_call(
        functools.partial(kernel, counts),
        out_shape=(
            jax.ShapeDtypeStruct((5, 1, rows, width), f32),
            jax.ShapeDtypeStruct((2, 1, rows, width), f32),
        ),
        in_specs=[pl.BlockSpec(memory_space=pltpu.HBM)] * 2,
        out_specs=[pl.BlockSpec(memory_space=pl.ANY)] * 2,
        scratch_shapes=[plane] * 6
        + [five] * 3
        + [plane] * 8
        + [pair] * 4
        + [packet] * 9
        + [mains] * 2
        + [
            pltpu.SemaphoreType.DMA((2, nw)),
            pltpu.SemaphoreType.DMA((KINDS, nw)),
            pltpu.SemaphoreType.DMA((KINDS, nw)),
            pltpu.SemaphoreType.DMA((4, chunks)),
            pltpu.SemaphoreType.DMA((4, chunks)),
        ],
        compiler_params=pltpu.CompilerParams(
            collective_id=0, has_side_effects=True, vmem_limit_bytes=48 * 1024 * 1024
        ),
    )(*(pltpu.with_memory_space_constraint(x, pltpu.HBM) for x in (images, stiffness)))


def solution(mesh):
    counts = tuple(mesh.shape[name] for name in ("sec", "row", "col"))
    spec = P("sec", "row", "col")
    out = P(None, "sec", "row", "col")
    return jax.shard_map(
        functools.partial(local, counts), mesh=mesh, in_specs=(spec, spec),
        out_specs=(out, out), check_vma=False,
    )
```
